32 devices in a mesh: groups: 2 (over y), ctx: 4 (over z), tp: 2 (over x), sub: 2 (over core).
Axes of the slice: x: 2, y: 2, z: 4, core: 2. Of those that a mesh axis runs over, the one named last changes fastest.
Arguments:
- queries: bfloat16 [3072, 8192], P(('groups', 'ctx'), ('tp', 'sub')), parts along dimension 0, may hold values from -200 to 200
- keys: bfloat16 [3072, 1024], P(('groups', 'ctx'), ('tp', 'sub')), parts along dimension 0, may hold values from -6 to 6
- values: bfloat16 [3072, 1024], P(('groups', 'ctx'), ('tp', 'sub')), parts along dimension 0, may hold values from -6 to 6
- segment_ids: int32 [3072], P(('groups', 'ctx')), parts along dimension 0, may hold values from 0 to 8, as said below
Outputs:
- attended: bfloat16 [3072, 8192], P(('groups', 'ctx'), ('tp', 'sub')), parts along dimension 0
The draws below stay inside these ranges and needn't reach their ends.
There are 2 independent parts, one for each index of `groups`. The reference program is written for one: setup_inputs(seed, part) draws one part's arguments, and reference() takes and returns one part's arrays. A program takes and returns all parts, laid end to end along the dimension named above; each array names one. Nothing has to cross between parts.
Inputs may be any that keep to these rules, and one draw needn't show every extreme that they name: segment_ids is 0 on the first 384 tokens; after them exactly 8 chains 1, 2, ..., 8 follow in order and fill the row, each a run of 96 to 192 tokens, one of them exactly 192.
All inputs are finite; a program needn't handle non-finite values.
Results may differ from the reference program's by a relative error of at most 0.0041.
Values may be sent and summed in bfloat16 or wider, within the bound.
No kernel may reach another device: no remote copies, remote signals or barrier semaphores. Data moves between devices by JAX's collectives and lax.ppermute only.
A program may use at most 64 MiB of HBM per device.

```python
import jax
import jax.numpy as jnp
from jax import lax

HEADS = 64
KV_HEADS = 8
HEAD_DIM = 128
GROUP = 8
TOKENS = 1536
PROMPT = 384
CHAIN = 192


def paired_draw(key):
    base_keys = jnp.clip(jax.random.normal(jax.random.fold_in(key, 12), (TOKENS, KV_HEADS, HEAD_DIM), jnp.float32), -6.0, 6.0)
    base_queries = jnp.clip(jax.random.normal(jax.random.fold_in(key, 11), (TOKENS, KV_HEADS, GROUP, HEAD_DIM), jnp.float32), -6.0, 6.0)
    keys_out = base_keys
    queries_out = base_queries
    queries_flat = queries_out.reshape(TOKENS, HEADS * HEAD_DIM).astype(jnp.bfloat16)
    keys_flat = keys_out.reshape(TOKENS, KV_HEADS * HEAD_DIM).astype(jnp.bfloat16)
    return (queries_flat, keys_flat)


def draw_queries(key, part):
    return paired_draw(key)[0]


def draw_keys(key, part):
    return paired_draw(key)[1]


def draw_segment_ids(key, part):
    quarter = CHAIN // 4
    middle = 3 * quarter
    shifts = jax.random.randint(jax.random.fold_in(key, 21), (4,), -quarter, quarter + 1)
    longest = jax.random.randint(jax.random.fold_in(key, 22), (), 0, 4)
    shifts = jnp.where(jnp.arange(4, dtype=jnp.int32) == longest, quarter, shifts)
    signs = jax.random.randint(jax.random.fold_in(key, 23), (4,), 0, 2) * 2 - 1
    shifts = shifts * signs
    lengths = jnp.stack([middle + shifts, middle - shifts], axis=1).reshape(8).astype(jnp.int32)
    bounds = PROMPT + jnp.cumsum(lengths)
    places = jnp.arange(TOKENS, dtype=jnp.int32)
    passed = jnp.sum((places[:, None] >= bounds[None, :]).astype(jnp.int32), axis=1)
    return jnp.where(places < PROMPT, 0, 1 + passed).astype(jnp.int32)


def shard_levels(key, shape, pieces, smallest, largest):
    factor_of, own = 1.0, jax.random.fold_in(key, 6)
    for position, parts in pieces:
        draws = jnp.exp(jax.random.uniform(jax.random.fold_in(own, position), (parts,), jnp.float32, smallest / len(pieces), largest / len(pieces)))
        factor_of = factor_of * jnp.repeat(draws, shape[position] // parts).reshape([-1 if axis == position else 1 for axis in range(len(shape))])
    return factor_of


def gaussian(stream_key, extent, width, reach, split=(), kind=jnp.bfloat16):
    values = jax.random.normal(stream_key, extent, jnp.float32) * width
    if len(split) > 0:
        values = shard_levels(stream_key, extent, split, -0.22, 0.18) * values
    return jnp.clip(values, min=-reach, max=reach).astype(kind)


def setup_inputs(seed: int = 0, part: int = 0) -> dict:
    arg_keys = jax.random.split(jax.random.key(seed), 5)
    part_keys = jax.random.split(jax.random.fold_in(arg_keys[4], part), 5)
    queries = draw_queries(jax.random.fold_in(jax.random.fold_in(arg_keys[4], part), 71), part)
    keys = draw_keys(jax.random.fold_in(jax.random.fold_in(arg_keys[4], part), 71), part)
    values = gaussian(part_keys[2], (TOKENS, KV_HEADS * HEAD_DIM), 1.0, 6.0, ((0, 4), (1, 4)))
    segment_ids = draw_segment_ids(jax.random.fold_in(jax.random.fold_in(arg_keys[4], part), 71), part)
    return dict(queries=queries, keys=keys, values=values, segment_ids=segment_ids)


def reference(queries, keys, values, segment_ids):
    scaling = HEAD_DIM ** -0.5
    block_rows = min(128, TOKENS)
    block_count = TOKENS // block_rows
    places = jnp.arange(TOKENS, dtype=jnp.int32)
    keys_all = keys.astype(jnp.float32).reshape(TOKENS, KV_HEADS, HEAD_DIM)
    values_all = values.astype(jnp.float32).reshape(TOKENS, KV_HEADS, HEAD_DIM)
    query_blocks = queries.reshape(block_count, block_rows, KV_HEADS, GROUP, HEAD_DIM)
    place_blocks = places.reshape(block_count, block_rows)
    segment_blocks = segment_ids.reshape(block_count, block_rows)

    def one_block(inputs):
        query_block, query_places, query_segments = inputs
        same = (segment_ids[None, :] == query_segments[:, None]) | (segment_ids[None, :] == 0)
        visible = (places[None, :] <= query_places[:, None]) & same
        scores = jnp.einsum("qhgd,khd->hgqk", query_block.astype(jnp.float32), keys_all) * scaling
        scores = jnp.where(visible[None, None], scores, -1e30)
        row_peak = jnp.max(scores, axis=-1, keepdims=True)
        weights = jnp.where(visible[None, None], jnp.exp(scores - row_peak), 0.0)
        row_total = jnp.sum(weights, axis=-1)
        rounded = lax.optimization_barrier(weights.astype(jnp.bfloat16))
        mixed = jnp.einsum("hgqk,khd->qhgd", rounded.astype(jnp.float32), values_all)
        mixed = mixed / jnp.transpose(row_total, (2, 0, 1))[..., None]
        return mixed.reshape(block_rows, HEADS * HEAD_DIM).astype(jnp.bfloat16)

    result = lax.map(one_block, (query_blocks, place_blocks, segment_blocks))
    return result.reshape(TOKENS, HEADS * HEAD_DIM)
```

```python
import functools

import jax
import jax.numpy as jnp
from jax import lax
from jax.experimental import pallas as pl
from jax.experimental.pallas import tpu as pltpu
from jax.sharding import PartitionSpec as P

HEAD_DIM = 128
GROUP = 8
LANES = 128
ROWS = 128
NEG = -1e30
EXP2_SCALE = 1.4426950408889634 * HEAD_DIM ** (-0.5)

VMEM = pl.BlockSpec(memory_space=pltpu.VMEM)
SMEM = pl.BlockSpec(memory_space=pltpu.SMEM)
HBM = pl.BlockSpec(memory_space=pltpu.HBM)


def dot_t(a, b):
    return lax.dot_general(a, b, (((1,), (1,)), ((), ())), preferred_element_type=jnp.float32)


def head_cols(kv_head):
    first = kv_head * GROUP * HEAD_DIM
    return [slice(first + g * HEAD_DIM, first + (g + 1) * HEAD_DIM) for g in range(GROUP)]


def stack(ref, rows, cols):
    return jnp.concatenate([ref[rows, c] for c in cols], axis=0)


def unstack(ref, rows, cols, value):
    for g, c in enumerate(cols):
        ref[rows, c] = value[g * ROWS : (g + 1) * ROWS].astype(ref.dtype)


def widen(lane_copies, width):
    whole = -(-width // LANES)
    return jnp.concatenate([lane_copies] * whole, axis=1)[:, :width]


def with_ones(wide, source, rows, heads):
    for h in range(heads):
        wide[0:rows, 2 * h * HEAD_DIM : (2 * h + 1) * HEAD_DIM] = source[0:rows, h * HEAD_DIM : (h + 1) * HEAD_DIM]


def fill_ones(wide, heads):
    for h in range(heads):
        wide[:, (2 * h + 1) * HEAD_DIM : (2 * h + 2) * HEAD_DIM] = jnp.ones((wide.shape[0], HEAD_DIM), jnp.bfloat16)


def fetch(source, target, sem):
    copy = pltpu.make_async_copy(source, target, sem)
    copy.start()
    return copy


def own_kernel(q_hbm, k_hbm, v_hbm, seg_ref, state_hbm, q_ref, k_ref, v_ref, state, bias, wide, in_sem, out_sem):
    count, width = q_ref.shape
    heads = k_ref.shape[1] // HEAD_DIM
    blocks = count // ROWS
    span = [slice(b * ROWS, (b + 1) * ROWS) for b in range(blocks)]
    get_k = fetch(k_hbm, k_ref, in_sem.at[blocks])
    get_q = [fetch(q_hbm.at[rows], q_ref.at[rows], in_sem.at[b]) for b, rows in enumerate(span)]
    get_v = fetch(v_hbm, v_ref, in_sem.at[blocks + 1])
    seg = seg_ref[...].astype(jnp.float32)
    for b in range(blocks):
        of_row = jnp.broadcast_to(seg[:, span[b]], (ROWS, ROWS)).T
        for t in range(b + 1):
            of_key = jnp.broadcast_to(seg[:, span[t]], (ROWS, ROWS))
            seen = (of_key == of_row) | (of_key == 0.0)
            if t == b:
                i = lax.broadcasted_iota(jnp.int32, (ROWS, ROWS), 0)
                j = lax.broadcasted_iota(jnp.int32, (ROWS, ROWS), 1)
                seen = seen & (j <= i)
            bias[span[b], span[t]] = jnp.where(seen, 0.0, NEG)
    fill_ones(wide, heads)
    get_k.wait()
    get_v.wait()
    with_ones(wide, v_ref, count, heads)
    lane = lax.broadcasted_iota(jnp.int32, (ROWS, LANES), 1)
    put = []
    for b in range(blocks):
        rows, keys = span[b], (b + 1) * ROWS
        get_q[b].wait()
        peaks = jnp.zeros((ROWS, LANES), jnp.float32)
        totals = jnp.ones((ROWS, LANES), jnp.float32)
        for h in range(heads):
            cols = head_cols(h)
            scores = dot_t(stack(q_ref, rows, cols), k_ref[0:keys, h * HEAD_DIM : (h + 1) * HEAD_DIM])
            scores = scores.reshape(GROUP, ROWS, keys) + bias[rows, 0:keys][None]
            peak = jnp.max(scores, axis=-1, keepdims=True)
            weights = jnp.exp2((scores - peak) * EXP2_SCALE).astype(jnp.bfloat16).reshape(GROUP * ROWS, keys)
            sums = jnp.dot(
                weights, wide[0:keys, 2 * h * HEAD_DIM : (2 * h + 2) * HEAD_DIM], preferred_element_type=jnp.float32
            )
            unstack(state, rows, cols, sums[:, :HEAD_DIM])
            for g in range(GROUP):
                here = lane == h * GROUP + g
                peaks = jnp.where(here, peak[g], peaks)
                totals = jnp.where(here, sums[g * ROWS : (g + 1) * ROWS, HEAD_DIM:], totals)
        state[rows, width : width + LANES] = peaks
        state[rows, width + LANES : width + 2 * LANES] = totals
        put.append(fetch(state.at[rows], state_hbm.at[rows], out_sem.at[b]))
    for copy in put:
        copy.wait()


def prompt_scores_kernel(place_ref, q_ref, k1_ref, k2_ref, k3_ref, w_ref, peak_ref):
    count = q_ref.shape[0]
    heads = k1_ref.shape[1] // HEAD_DIM

    def compute(k_ref):
        for h in range(heads):
            cols = head_cols(h)
            for b in range(count // ROWS):
                rows = slice(b * ROWS, (b + 1) * ROWS)
                scores = dot_t(stack(q_ref, rows, cols), k_ref[:, h * HEAD_DIM : (h + 1) * HEAD_DIM])
                peak = jnp.max(scores, axis=-1, keepdims=True)
                weights = jnp.exp2((scores - peak) * EXP2_SCALE).astype(jnp.bfloat16)
                first = (h * (count // ROWS) + b) * GROUP * ROWS
                w_ref[first : first + GROUP * ROWS, :] = weights
                unstack(peak_ref, rows, cols, jnp.broadcast_to(peak, (GROUP * ROWS, LANES)))

    for place, k_ref in ((1, k1_ref), (2, k2_ref), (3, k3_ref)):
        pl.when(place_ref[0] == place)(functools.partial(compute, k_ref))


def tail_kernel(
    place_ref, q_ref, t2_ref, t3_ref, seg_ref, state_hbm, ppeak_ref,
    acc_ref, total_ref, factor_ref, state, tail, wide, in_sem,
):
    count, width = q_ref.shape
    heads = width // HEAD_DIM // GROUP
    half = count // 2
    blocks = count // ROWS
    place = place_ref[0]
    span = [slice(b * ROWS, (b + 1) * ROWS) for b in range(blocks)]
    get = [fetch(state_hbm.at[rows], state.at[rows], in_sem.at[b]) for b, rows in enumerate(span)]

    @pl.when(place == 2)
    def _():
        tail[...] = t2_ref[...]

    @pl.when(place == 3)
    def _():
        tail[...] = t3_ref[...]

    def merge(with_tail):
        if with_tail:
            fill_ones(wide, heads)
            for h in range(heads):
                wide[:, 2 * h * HEAD_DIM : (2 * h + 1) * HEAD_DIM] = tail[
                    half : 2 * half, h * HEAD_DIM : (h + 1) * HEAD_DIM
                ]
            of_keys = tail[2 * half : 2 * half + 16, :].astype(jnp.float32)[0:1, 0:half]
            seg = seg_ref[...].astype(jnp.float32)
        for b in range(blocks):
            rows = span[b]
            get[b].wait()
            low = b * ROWS // 64 * 64
            tailed = with_tail and low < half
            keys = half - low
            if tailed:
                of_row = jnp.broadcast_to(seg[:, rows], (ROWS, ROWS)).T
                seen = widen(of_row, half)[:, low:] == jnp.broadcast_to(of_keys, (ROWS, half))[:, low:]
                bias = jnp.where(seen, 0.0, NEG)
            for h in range(heads):
                cols = head_cols(h)
                first = width + h * GROUP
                own = jnp.concatenate(
                    [jnp.broadcast_to(state[rows, first + g : first + g + 1], (ROWS, LANES)) for g in range(GROUP)], axis=0
                )
                first = width + LANES + h * GROUP
                total = jnp.concatenate(
                    [jnp.broadcast_to(state[rows, first + g : first + g + 1], (ROWS, LANES)) for g in range(GROUP)], axis=0
                )
                prompt = jnp.where(place > 0, stack(ppeak_ref, rows, cols), NEG)
                peak = jnp.maximum(own, prompt)
                if tailed:
                    scores = dot_t(stack(q_ref, rows, cols), tail[low:half, h * HEAD_DIM : (h + 1) * HEAD_DIM])
                    scores = scores.reshape(GROUP, ROWS, keys) + bias[None]
                    scores = scores.reshape(GROUP * ROWS, keys)
                    peak = jnp.maximum(peak, jnp.max(scores, axis=-1, keepdims=True))
                    weights = jnp.exp2((scores - widen(peak, keys)) * EXP2_SCALE).astype(jnp.bfloat16)
                    sums = jnp.dot(
                        weights,
                        wide[low:half, 2 * h * HEAD_DIM : (2 * h + 2) * HEAD_DIM],
                        preferred_element_type=jnp.float32,
                    )
                scale = jnp.exp2((own - peak) * EXP2_SCALE)
                acc = stack(state, rows, cols) * scale
                total = total * scale
                if tailed:
                    acc = acc + sums[:, :HEAD_DIM]
                    total = total + sums[:, HEAD_DIM:]
                unstack(acc_ref, rows, cols, acc)
                unstack(total_ref, rows, cols, total)
                unstack(factor_ref, rows, cols, jnp.exp2((prompt - peak) * EXP2_SCALE))

    pl.when(place <= 1)(functools.partial(merge, False))
    pl.when(place > 1)(functools.partial(merge, True))


def final_kernel(place_ref, w_ref, v1_ref, v2_ref, v3_ref, acc_ref, total_ref, factor_ref, out_ref, wide, staged, sem):
    count = acc_ref.shape[0]
    heads = acc_ref.shape[1] // HEAD_DIM // GROUP
    place = place_ref[0]
    span = GROUP * HEAD_DIM

    def copy(h, b):
        box = (pl.ds(b * ROWS, ROWS), pl.ds(h * span, span))
        return pltpu.make_async_copy(staged.at[box], out_ref.at[box], sem.at[h, b])

    blocks = [(h, b) for h in range(heads) for b in range(count // ROWS)]

    @pl.when(place == 0)
    def _():
        for h, b in blocks:
            box = (slice(b * ROWS, (b + 1) * ROWS), slice(h * span, (h + 1) * span))
            staged[box] = (acc_ref[box] / total_ref[box]).astype(jnp.bfloat16)
            copy(h, b).start()

    @pl.when(place > 0)
    def _():
        fill_ones(wide, heads)
        for where, v_ref in ((1, v1_ref), (2, v2_ref), (3, v3_ref)):
            pl.when(place == where)(functools.partial(with_ones, wide, v_ref, count, heads))
        for h, b in blocks:
            cols = head_cols(h)
            rows = slice(b * ROWS, (b + 1) * ROWS)
            first = (h * (count // ROWS) + b) * GROUP * ROWS
            sums = jnp.dot(
                w_ref[first : first + GROUP * ROWS, :],
                wide[:, 2 * h * HEAD_DIM : (2 * h + 2) * HEAD_DIM],
                preferred_element_type=jnp.float32,
            )
            factor = stack(factor_ref, rows, cols)
            acc = stack(acc_ref, rows, cols) + sums[:, :HEAD_DIM] * factor
            total = stack(total_ref, rows, cols) + sums[:, HEAD_DIM:] * factor
            unstack(staged, rows, cols, acc / total)
            copy(h, b).start()

    for h, b in blocks:
        copy(h, b).wait()


def cost(flops, moved):
    return pl.CostEstimate(flops=flops, bytes_accessed=moved, transcendentals=0)


def prompt_block_path(queries, keys, values, segment_ids):
    count, kv_width = keys.shape
    width = queries.shape[1]
    half = count // 2
    blocks = count // ROWS
    place = lax.axis_index("ctx").astype(jnp.int32)
    where = place.reshape(1)
    seg_row = segment_ids.reshape(1, count)

    keys_2 = lax.ppermute(keys, "ctx", [(0, 2)])
    values_2 = lax.ppermute(values, "ctx", [(0, 2)])
    seg_tail = jnp.broadcast_to(
        jnp.pad(segment_ids[half:].astype(jnp.bfloat16), (0, kv_width - half))[None], (16, kv_width)
    )
    tail = jnp.concatenate([keys[half:], values[half:], seg_tail], axis=0)
    mixed = jnp.where(place == 0, jnp.concatenate([values, seg_tail], axis=0), tail)
    tail_3 = lax.ppermute(mixed, "ctx", [(2, 3)])

    stat = jax.ShapeDtypeStruct(queries.shape, jnp.float32)
    state_shape = (count, width + 2 * LANES)
    state = pl.pallas_call(
        own_kernel,
        out_shape=jax.ShapeDtypeStruct(state_shape, jnp.float32),
        in_specs=[HBM] * 3 + [VMEM],
        out_specs=HBM,
        scratch_shapes=[
            pltpu.VMEM(queries.shape, jnp.bfloat16),
            pltpu.VMEM(keys.shape, jnp.bfloat16),
            pltpu.VMEM(keys.shape, jnp.bfloat16),
            pltpu.VMEM(state_shape, jnp.float32),
            pltpu.VMEM((count, count), jnp.float32),
            pltpu.VMEM((count, 2 * kv_width), jnp.bfloat16),
            pltpu.SemaphoreType.DMA((blocks + 2,)),
            pltpu.SemaphoreType.DMA((blocks,)),
        ],
        compiler_params=pltpu.CompilerParams(vmem_limit_bytes=14 << 20),
        cost_estimate=cost(4 * count * count * width, 0),
        name="own",
    )(queries, keys, values, seg_row)

    keys_3 = lax.ppermute(keys_2, "ctx", [(2, 3)])
    keys_1 = lax.ppermute(keys_2, "ctx", [(2, 1)])
    mixed, state = lax.optimization_barrier((mixed, state))
    from_left = lax.ppermute(mixed, "ctx", [(0, 1), (1, 2)])
    values_3 = lax.ppermute(values_2, "ctx", [(2, 3)])

    weights, prompt_peak = pl.pallas_call(
        prompt_scores_kernel,
        out_shape=(jax.ShapeDtypeStruct((count * width // HEAD_DIM, count), jnp.bfloat16), stat),
        in_specs=[SMEM] + [VMEM] * 4,
        out_specs=(VMEM,) * 2,
        compiler_params=pltpu.CompilerParams(vmem_limit_bytes=8 << 20),
        cost_estimate=cost(1, 1),
        name="prompt_scores",
    )(where, queries, keys_1, keys_2, keys_3)

    acc, total, factor = pl.pallas_call(
        tail_kernel,
        out_shape=(stat, stat, stat),
        in_specs=[SMEM] + [VMEM] * 4 + [HBM, VMEM],
        out_specs=(VMEM,) * 3,
        scratch_shapes=[
            pltpu.VMEM(state_shape, jnp.float32),
            pltpu.VMEM(mixed.shape, jnp.bfloat16),
            pltpu.VMEM((half, 2 * kv_width), jnp.bfloat16),
            pltpu.SemaphoreType.DMA((blocks,)),
        ],
        compiler_params=pltpu.CompilerParams(vmem_limit_bytes=10 << 20),
        cost_estimate=cost(1, 1),
        name="tail",
    )(where, queries, from_left, tail_3, seg_row, state, prompt_peak)

    return pl.pallas_call(
        final_kernel,
        out_shape=jax.ShapeDtypeStruct(queries.shape, jnp.bfloat16),
        in_specs=[SMEM] + [VMEM] * 7,
        out_specs=pl.BlockSpec(memory_space=pl.ANY),
        scratch_shapes=[
            pltpu.VMEM((count, 2 * kv_width), jnp.bfloat16),
            pltpu.VMEM(queries.shape, jnp.bfloat16),
            pltpu.SemaphoreType.DMA((kv_width // HEAD_DIM, blocks)),
        ],
        compiler_params=pltpu.CompilerParams(vmem_limit_bytes=8 << 20),
        cost_estimate=cost(1, 1),
        name="final",
    )(where, weights, from_left, values_2, values_3, acc, total, factor)


def attend_block(
    running,
    key_block,
    value_block,
    segment_block,
    first_row,
    query_heads,
    query_places,
    query_segment,
):
    number = key_block.shape[0]
    heads_here = key_block.shape[1] // HEAD_DIM
    key_places = first_row + jnp.arange(number, dtype=jnp.int32)
    same = (segment_block[None, :] == query_segment[:, None]) | (segment_block[None, :] == 0)
    visible = (key_places[None, :] <= query_places[:, None]) & same
    key_heads = key_block.reshape(number, heads_here, HEAD_DIM)
    value_heads = value_block.reshape(number, heads_here, HEAD_DIM)

    def compute(state):
        row_peak, row_total, weighted = state
        scores = jnp.einsum(
            "qhgd,khd->hgqk", query_heads, key_heads, preferred_element_type=jnp.float32
        ) * HEAD_DIM ** (-0.5)
        scores = jnp.where(visible[None, None], scores, -1e30)
        new_peak = jnp.maximum(row_peak, jnp.max(scores, axis=-1))
        factor = jnp.exp(row_peak - new_peak)
        weights = jnp.where(visible[None, None], jnp.exp(scores - new_peak[..., None]), 0.0)
        new_total = row_total * factor + jnp.sum(weights, axis=-1)
        added = jnp.einsum(
            "hgqk,khd->hgqd",
            weights.astype(jnp.bfloat16),
            value_heads,
            preferred_element_type=jnp.float32,
        )
        return (new_peak, new_total, weighted * factor[..., None] + added)

    return lax.cond(jnp.any(visible), compute, lambda state: state, running)


def gathered_path(queries, keys, values, segment_ids):
    row_count = queries.shape[0]
    heads_here = keys.shape[1] // HEAD_DIM
    my_index = lax.axis_index("ctx")
    query_places = my_index * row_count + jnp.arange(row_count, dtype=jnp.int32)
    query_heads = queries.reshape(row_count, heads_here, GROUP, HEAD_DIM)
    initial = (
        jnp.full((heads_here, GROUP, row_count), -1e30, jnp.float32),
        jnp.zeros((heads_here, GROUP, row_count), jnp.float32),
        jnp.zeros((heads_here, GROUP, row_count, HEAD_DIM), jnp.float32),
    )
    key_all = lax.all_gather(keys, "ctx", axis=0, tiled=True)
    value_all = lax.all_gather(values, "ctx", axis=0, tiled=True)
    segment_all = lax.all_gather(segment_ids, "ctx", axis=0, tiled=True)
    blocks = max(1, key_all.shape[0] // row_count)
    width_rows = key_all.shape[0] // blocks

    def turn(number, state):
        offset = number * width_rows
        key_part = lax.dynamic_slice_in_dim(key_all, offset, width_rows, 0)
        value_part = lax.dynamic_slice_in_dim(value_all, offset, width_rows, 0)
        segment_part = lax.dynamic_slice_in_dim(segment_all, offset, width_rows, 0)
        return attend_block(
            state, key_part, value_part, segment_part, offset, query_heads, query_places, segment_ids
        )

    row_peak, row_total, weighted = lax.fori_loop(0, blocks, turn, initial)
    mixed = weighted / row_total[..., None]
    mixed = jnp.transpose(mixed, (2, 0, 1, 3)).reshape(row_count, heads_here * GROUP * HEAD_DIM)
    return mixed.astype(jnp.bfloat16)


def per_device(parts, queries, keys, values, segment_ids):
    rows = queries.shape[0]
    tokens = rows * parts
    prompt, chain = tokens // 4, tokens // 8
    if parts == 4 and prompt == rows and 2 * chain == rows and rows % ROWS == 0 and keys.shape[1] >= chain:
        return prompt_block_path(queries, keys, values, segment_ids)
    return gathered_path(queries, keys, values, segment_ids)


def solution(mesh):
    placed = (
        P(("groups", "ctx"), ("tp", "sub")),
        P(("groups", "ctx"), ("tp", "sub")),
        P(("groups", "ctx"), ("tp", "sub")),
        P(("groups", "ctx")),
    )
    return jax.shard_map(
        functools.partial(per_device, mesh.shape["ctx"]),
        mesh=mesh,
        in_specs=placed,
        out_specs=P(("groups", "ctx"), ("tp", "sub")),
        check_vma=False,
    )
```

```python
import functools

import jax
import jax.numpy as jnp
from jax import lax
from jax.experimental import pallas as pl
from jax.experimental.pallas import tpu as pltpu
from jax.sharding import PartitionSpec as P

HEAD_DIM = 128
GROUP = 8
LANES = 128
ROWS = 128
NEG = -1e30
EXP2_SCALE = 1.4426950408889634 * HEAD_DIM ** (-0.5)

VMEM = pl.BlockSpec(memory_space=pltpu.VMEM)
SMEM = pl.BlockSpec(memory_space=pltpu.SMEM)
HBM = pl.BlockSpec(memory_space=pltpu.HBM)


def dot_t(a, b):
    return lax.dot_general(a, b, (((1,), (1,)), ((), ())), preferred_element_type=jnp.float32)


def head_cols(kv_head):
    first = kv_head * GROUP * HEAD_DIM
    return [slice(first + g * HEAD_DIM, first + (g + 1) * HEAD_DIM) for g in range(GROUP)]


def stack(ref, rows, cols):
    return jnp.concatenate([ref[rows, c] for c in cols], axis=0)


def unstack(ref, rows, cols, value):
    for g, c in enumerate(cols):
        ref[rows, c] = value[g * ROWS : (g + 1) * ROWS].astype(ref.dtype)


def widen(lane_copies, width):
    whole = -(-width // LANES)
    return jnp.concatenate([lane_copies] * whole, axis=1)[:, :width]


def with_ones(wide, source, rows, heads):
    for h in range(heads):
        wide[0:rows, 2 * h * HEAD_DIM : (2 * h + 1) * HEAD_DIM] = source[0:rows, h * HEAD_DIM : (h + 1) * HEAD_DIM]


def fill_ones(wide, heads):
    for h in range(heads):
        wide[:, (2 * h + 1) * HEAD_DIM : (2 * h + 2) * HEAD_DIM] = jnp.ones((wide.shape[0], HEAD_DIM), jnp.bfloat16)


def fetch(source, target, sem):
    copy = pltpu.make_async_copy(source, target, sem)
    copy.start()
    return copy


def pack_kernel(place_ref, k_hbm, v_hbm, seg_hbm, mixed_ref, seg_ref, sem):
    count = k_hbm.shape[0]
    half = count // 2
    place = place_ref[0]
    low, high = pl.ds(0, half), pl.ds(half, half)
    get_seg = fetch(seg_hbm, seg_ref, sem.at[2])

    @pl.when(place == 0)
    def _():
        fetch(v_hbm.at[low], mixed_ref.at[low], sem.at[0])

    @pl.when(place > 0)
    def _():
        fetch(k_hbm.at[high], mixed_ref.at[low], sem.at[0])

    other = fetch(v_hbm.at[high], mixed_ref.at[high], sem.at[1])
    get_seg.wait()
    seg = seg_ref[...].reshape(1, count).astype(jnp.float32)[:, half:]
    pltpu.make_async_copy(k_hbm.at[high], mixed_ref.at[low], sem.at[0]).wait()

    @pl.when(place > 0)
    def _():
        first = lax.broadcasted_iota(jnp.int32, (16, half), 0) == 0
        old = mixed_ref[0:16, 0:half].astype(jnp.float32)
        mixed_ref[0:16, 0:half] = jnp.where(first, jnp.broadcast_to(seg, (16, half)), old).astype(jnp.bfloat16)

    other.wait()


def own_kernel(q_hbm, k_hbm, v_hbm, seg_hbm, state, q_ref, k_ref, v_ref, seg_ref, bias, wide, in_sem):
    count, width = q_ref.shape
    heads = k_ref.shape[1] // HEAD_DIM
    blocks = count // ROWS
    span = [slice(b * ROWS, (b + 1) * ROWS) for b in range(blocks)]
    get_seg = fetch(seg_hbm, seg_ref, in_sem.at[blocks + 2])
    get_k = fetch(k_hbm, k_ref, in_sem.at[blocks])
    get_q = [fetch(q_hbm.at[rows], q_ref.at[rows], in_sem.at[b]) for b, rows in enumerate(span)]
    get_v = fetch(v_hbm, v_ref, in_sem.at[blocks + 1])
    get_seg.wait()
    seg = seg_ref[...].reshape(1, count).astype(jnp.float32)
    for b in range(blocks):
        of_row = jnp.broadcast_to(seg[:, span[b]], (ROWS, ROWS)).T
        for t in range(b + 1):
            of_key = jnp.broadcast_to(seg[:, span[t]], (ROWS, ROWS))
            seen = (of_key == of_row) | (of_key == 0.0)
            if t == b:
                i = lax.broadcasted_iota(jnp.int32, (ROWS, ROWS), 0)
                j = lax.broadcasted_iota(jnp.int32, (ROWS, ROWS), 1)
                seen = seen & (j <= i)
            bias[span[b], span[t]] = jnp.where(seen, 0.0, NEG)
    fill_ones(wide, heads)
    get_k.wait()
    get_v.wait()
    with_ones(wide, v_ref, count, heads)
    lane = lax.broadcasted_iota(jnp.int32, (ROWS, LANES), 1)
    for b in range(blocks):
        rows, keys = span[b], (b + 1) * ROWS
        get_q[b].wait()
        peaks = jnp.zeros((ROWS, LANES), jnp.float32)
        totals = jnp.ones((ROWS, LANES), jnp.float32)
        for h in range(heads):
            cols = head_cols(h)
            scores = dot_t(stack(q_ref, rows, cols), k_ref[0:keys, h * HEAD_DIM : (h + 1) * HEAD_DIM])
            scores = scores.reshape(GROUP, ROWS, keys) + bias[rows, 0:keys][None]
            peak = jnp.max(scores, axis=-1, keepdims=True)
            weights = jnp.exp2((scores - peak) * EXP2_SCALE).astype(jnp.bfloat16).reshape(GROUP * ROWS, keys)
            sums = jnp.dot(
                weights, wide[0:keys, 2 * h * HEAD_DIM : (2 * h + 2) * HEAD_DIM], preferred_element_type=jnp.float32
            )
            unstack(state, rows, cols, sums[:, :HEAD_DIM] / sums[:, HEAD_DIM:])
            for g in range(GROUP):
                here = lane == h * GROUP + g
                peaks = jnp.where(here, peak[g], peaks)
                totals = jnp.where(here, sums[g * ROWS : (g + 1) * ROWS, HEAD_DIM:], totals)
        state[rows, width : width + LANES] = peaks
        state[rows, width + LANES : width + 2 * LANES] = totals


def prompt_scores_kernel(place_ref, q_ref, k1_ref, k2_ref, k3_ref, w_ref, peak_ref):
    count = q_ref.shape[0]
    heads = k1_ref.shape[1] // HEAD_DIM
    lane = lax.broadcasted_iota(jnp.int32, (ROWS, LANES), 1)

    def compute(k_ref):
        for b in range(count // ROWS):
            rows = slice(b * ROWS, (b + 1) * ROWS)
            peaks = jnp.zeros((ROWS, LANES), jnp.float32)
            for h in range(heads):
                cols = head_cols(h)
                scores = dot_t(stack(q_ref, rows, cols), k_ref[:, h * HEAD_DIM : (h + 1) * HEAD_DIM])
                peak = jnp.max(scores, axis=-1, keepdims=True)
                weights = jnp.exp2((scores - peak) * EXP2_SCALE).astype(jnp.bfloat16)
                first = (h * (count // ROWS) + b) * GROUP * ROWS
                w_ref[first : first + GROUP * ROWS, :] = weights
                for g in range(GROUP):
                    peaks = jnp.where(lane == h * GROUP + g, peak[g * ROWS : (g + 1) * ROWS], peaks)
            peak_ref[rows, :] = peaks

    for place, k_ref in ((1, k1_ref), (2, k2_ref), (3, k3_ref)):
        pl.when(place_ref[0] == place)(functools.partial(compute, k_ref))


def column(stats, index):
    return jnp.broadcast_to(stats[:, index : index + 1], (stats.shape[0], LANES))


def tail_kernel(place_ref, q_ref, t2_ref, t3_ref, seg_ref, state_in, state, tail, wide):
    count, width = q_ref.shape
    heads = width // HEAD_DIM // GROUP
    half = count // 2
    place = place_ref[0]

    @pl.when(place == 2)
    def _():
        tail[...] = t2_ref[...]

    @pl.when(place == 3)
    def _():
        tail[...] = t3_ref[...]

    @pl.when(place > 1)
    def _():
        fill_ones(wide, heads)
        for h in range(heads):
            wide[:, 2 * h * HEAD_DIM : (2 * h + 1) * HEAD_DIM] = tail[half : 2 * half, h * HEAD_DIM : (h + 1) * HEAD_DIM]
        of_keys = tail[0:16, 0:half].astype(jnp.float32)[0:1]
        of_keys = jnp.where(lax.broadcasted_iota(jnp.int32, (1, half), 1) == 0, -1.0, of_keys)
        seg = seg_ref[...].reshape(1, count).astype(jnp.float32)
        for start in range(0, half, ROWS):
            size = min(ROWS, half - start)
            low = start // 64 * 64
            keys = half - low
            rows = slice(start, start + size)
            of_row = jnp.broadcast_to(seg[:, start : start + ROWS], (ROWS, ROWS)).T[0:size]
            seen = widen(of_row, half)[:, low:] == jnp.broadcast_to(of_keys, (size, half))[:, low:]
            bias = jnp.where(seen, 0.0, NEG)
            lane = lax.broadcasted_iota(jnp.int32, (size, LANES), 1)
            old_peaks = state_in[rows, width : width + LANES]
            old_totals = state_in[rows, width + LANES : width + 2 * LANES]
            peaks, totals = old_peaks, old_totals
            for h in range(heads):
                cols = head_cols(h)
                queries = jnp.concatenate([q_ref[rows, c] for c in cols], axis=0)
                scores = dot_t(queries, tail[low:half, h * HEAD_DIM : (h + 1) * HEAD_DIM])
                scores = (scores.reshape(GROUP, size, keys) + bias[None]).reshape(GROUP * size, keys)
                own = jnp.concatenate([column(old_peaks, h * GROUP + g) for g in range(GROUP)], axis=0)
                peak = jnp.maximum(own, jnp.max(scores, axis=-1, keepdims=True))
                weights = jnp.exp2((scores - widen(peak, keys)) * EXP2_SCALE).astype(jnp.bfloat16)
                sums = jnp.dot(
                    weights,
                    wide[low:half, 2 * h * HEAD_DIM : (2 * h + 2) * HEAD_DIM],
                    preferred_element_type=jnp.float32,
                )
                total = jnp.concatenate([column(old_totals, h * GROUP + g) for g in range(GROUP)], axis=0)
                total = total * jnp.exp2((own - peak) * EXP2_SCALE)
                acc = jnp.concatenate([state_in[rows, c] for c in cols], axis=0) * total + sums[:, :HEAD_DIM]
                total = total + sums[:, HEAD_DIM:]
                acc = acc / total
                for g, c in enumerate(cols):
                    mine = slice(g * size, (g + 1) * size)
                    state[rows, c] = acc[mine]
                    here = lane == h * GROUP + g
                    peaks = jnp.where(here, peak[mine], peaks)
                    totals = jnp.where(here, total[mine], totals)
            state[rows, width : width + LANES] = peaks
            state[rows, width + LANES : width + 2 * LANES] = totals


def final_kernel(place_ref, w_ref, v1_ref, v2_ref, v3_ref, state, ppeak_ref, out_ref, wide, staged, sem):
    count, width = staged.shape
    heads = width // HEAD_DIM // GROUP
    place = place_ref[0]
    span = GROUP * HEAD_DIM

    def copy(h, b):
        box = (pl.ds(b * ROWS, ROWS), pl.ds(h * span, span))
        return pltpu.make_async_copy(staged.at[box], out_ref.at[box], sem.at[h, b])

    blocks = [(h, b) for b in range(count // ROWS) for h in range(heads)]

    @pl.when(place == 0)
    def _():
        for h, b in blocks:
            box = (slice(b * ROWS, (b + 1) * ROWS), slice(h * span, (h + 1) * span))
            staged[box] = state[box].astype(jnp.bfloat16)
            copy(h, b).start()

    @pl.when(place > 0)
    def _():
        fill_ones(wide, heads)
        for where, v_ref in ((1, v1_ref), (2, v2_ref), (3, v3_ref)):
            pl.when(place == where)(functools.partial(with_ones, wide, v_ref, count, heads))
        for h, b in blocks:
            cols = head_cols(h)
            rows = slice(b * ROWS, (b + 1) * ROWS)
            own, prompt = state[rows, width : width + LANES], ppeak_ref[rows, :]
            peak = jnp.maximum(own, prompt)
            factors = jnp.exp2((prompt - peak) * EXP2_SCALE)
            totals = state[rows, width + LANES : width + 2 * LANES] * jnp.exp2((own - peak) * EXP2_SCALE)
            first = (h * (count // ROWS) + b) * GROUP * ROWS
            sums = jnp.dot(
                w_ref[first : first + GROUP * ROWS, :],
                wide[:, 2 * h * HEAD_DIM : (2 * h + 2) * HEAD_DIM],
                preferred_element_type=jnp.float32,
            )
            for g, c in enumerate(cols):
                mine = slice(g * ROWS, (g + 1) * ROWS)
                total, factor = column(totals, h * GROUP + g), column(factors, h * GROUP + g)
                acc = state[rows, c] * total + sums[mine, :HEAD_DIM] * factor
                staged[rows, c] = (acc / (total + sums[mine, HEAD_DIM:] * factor)).astype(jnp.bfloat16)
            copy(h, b).start()

    for h, b in blocks:
        copy(h, b).wait()


def params(mebibytes):
    return pltpu.CompilerParams(vmem_limit_bytes=mebibytes << 20)


def cost(flops):
    return pl.CostEstimate(flops=flops, bytes_accessed=1, transcendentals=0)


def prompt_block_path(queries, keys, values, segment_ids):
    count, kv_width = keys.shape
    width = queries.shape[1]
    half = count // 2
    blocks = count // ROWS
    place = lax.axis_index("ctx").astype(jnp.int32).reshape(1)
    in_hbm = [pltpu.with_memory_space_constraint(x, pltpu.HBM) for x in (queries, keys, values, segment_ids)]

    keys_2 = lax.ppermute(keys, "ctx", [(0, 2)])
    values_2 = lax.ppermute(values, "ctx", [(0, 2)])
    mixed_shape = jax.ShapeDtypeStruct(keys.shape, jnp.bfloat16)
    mixed = pl.pallas_call(
        pack_kernel,
        out_shape=mixed_shape,
        in_specs=[SMEM] + [HBM] * 3,
        out_specs=VMEM,
        scratch_shapes=[pltpu.VMEM(segment_ids.shape, jnp.int32), pltpu.SemaphoreType.DMA((3,))],
        compiler_params=params(2),
        cost_estimate=cost(1),
        name="pack",
    )(place, *in_hbm[1:])
    tail_3 = lax.ppermute(mixed, "ctx", [(2, 3)])

    state_shape = jax.ShapeDtypeStruct((count, width + 2 * LANES), jnp.float32)
    state = pl.pallas_call(
        own_kernel,
        out_shape=state_shape,
        in_specs=[HBM] * 4,
        out_specs=VMEM,
        scratch_shapes=[
            pltpu.VMEM(queries.shape, jnp.bfloat16),
            pltpu.VMEM(keys.shape, jnp.bfloat16),
            pltpu.VMEM(keys.shape, jnp.bfloat16),
            pltpu.VMEM(segment_ids.shape, jnp.int32),
            pltpu.VMEM((count, count), jnp.float32),
            pltpu.VMEM((count, 2 * kv_width), jnp.bfloat16),
            pltpu.SemaphoreType.DMA((blocks + 3,)),
        ],
        compiler_params=params(10),
        cost_estimate=cost(16 * count * count * width),
        name="own",
    )(*in_hbm)

    keys_2, state = lax.optimization_barrier((keys_2, state))
    keys_3 = lax.ppermute(keys_2, "ctx", [(2, 3)])
    keys_1 = lax.ppermute(keys_2, "ctx", [(2, 1)])
    mixed, state = lax.optimization_barrier((mixed, state))
    from_left = lax.ppermute(mixed, "ctx", [(0, 1), (1, 2)])
    values_2, tail_3 = lax.optimization_barrier((values_2, tail_3))
    values_3 = lax.ppermute(values_2, "ctx", [(2, 3)])

    weights, prompt_peak = pl.pallas_call(
        prompt_scores_kernel,
        out_shape=(
            jax.ShapeDtypeStruct((count * width // HEAD_DIM, count), jnp.bfloat16),
            jax.ShapeDtypeStruct((count, LANES), jnp.float32),
        ),
        in_specs=[SMEM] + [VMEM] * 4,
        out_specs=(VMEM,) * 2,
        compiler_params=params(8),
        cost_estimate=cost(1),
        name="prompt_scores",
    )(place, queries, keys_1, keys_2, keys_3)

    state = pl.pallas_call(
        tail_kernel,
        out_shape=state_shape,
        in_specs=[SMEM] + [VMEM] * 5,
        out_specs=VMEM,
        scratch_shapes=[pltpu.VMEM(mixed.shape, jnp.bfloat16), pltpu.VMEM((half, 2 * kv_width), jnp.bfloat16)],
        input_output_aliases={5: 0},
        compiler_params=params(8),
        cost_estimate=cost(1),
        name="tail",
    )(place, queries, from_left, tail_3, segment_ids, state)

    return pl.pallas_call(
        final_kernel,
        out_shape=jax.ShapeDtypeStruct(queries.shape, jnp.bfloat16),
        in_specs=[SMEM] + [VMEM] * 6,
        out_specs=pl.BlockSpec(memory_space=pl.ANY),
        scratch_shapes=[
            pltpu.VMEM((count, 2 * kv_width), jnp.bfloat16),
            pltpu.VMEM(queries.shape, jnp.bfloat16),
            pltpu.SemaphoreType.DMA((kv_width // HEAD_DIM, blocks)),
        ],
        compiler_params=params(8),
        cost_estimate=cost(1),
        name="final",
    )(place, weights, from_left, values_2, values_3, state, prompt_peak)


def attend_block(
    running,
    key_block,
    value_block,
    segment_block,
    first_row,
    query_heads,
    query_places,
    query_segment,
):
    number = key_block.shape[0]
    heads_here = key_block.shape[1] // HEAD_DIM
    key_places = first_row + jnp.arange(number, dtype=jnp.int32)
    same = (segment_block[None, :] == query_segment[:, None]) | (segment_block[None, :] == 0)
    visible = (key_places[None, :] <= query_places[:, None]) & same
    key_heads = key_block.reshape(number, heads_here, HEAD_DIM)
    value_heads = value_block.reshape(number, heads_here, HEAD_DIM)

    def compute(state):
        row_peak, row_total, weighted = state
        scores = jnp.einsum(
            "qhgd,khd->hgqk", query_heads, key_heads, preferred_element_type=jnp.float32
        ) * HEAD_DIM ** (-0.5)
        scores = jnp.where(visible[None, None], scores, -1e30)
        new_peak = jnp.maximum(row_peak, jnp.max(scores, axis=-1))
        factor = jnp.exp(row_peak - new_peak)
        weights = jnp.where(visible[None, None], jnp.exp(scores - new_peak[..., None]), 0.0)
        new_total = row_total * factor + jnp.sum(weights, axis=-1)
        added = jnp.einsum(
            "hgqk,khd->hgqd",
            weights.astype(jnp.bfloat16),
            value_heads,
            preferred_element_type=jnp.float32,
        )
        return (new_peak, new_total, weighted * factor[..., None] + added)

    return lax.cond(jnp.any(visible), compute, lambda state: state, running)


def gathered_path(queries, keys, values, segment_ids):
    row_count = queries.shape[0]
    heads_here = keys.shape[1] // HEAD_DIM
    my_index = lax.axis_index("ctx")
    query_places = my_index * row_count + jnp.arange(row_count, dtype=jnp.int32)
    query_heads = queries.reshape(row_count, heads_here, GROUP, HEAD_DIM)
    initial = (
        jnp.full((heads_here, GROUP, row_count), -1e30, jnp.float32),
        jnp.zeros((heads_here, GROUP, row_count), jnp.float32),
        jnp.zeros((heads_here, GROUP, row_count, HEAD_DIM), jnp.float32),
    )
    key_all = lax.all_gather(keys, "ctx", axis=0, tiled=True)
    value_all = lax.all_gather(values, "ctx", axis=0, tiled=True)
    segment_all = lax.all_gather(segment_ids, "ctx", axis=0, tiled=True)
    blocks = max(1, key_all.shape[0] // row_count)
    width_rows = key_all.shape[0] // blocks

    def turn(number, state):
        offset = number * width_rows
        key_part = lax.dynamic_slice_in_dim(key_all, offset, width_rows, 0)
        value_part = lax.dynamic_slice_in_dim(value_all, offset, width_rows, 0)
        segment_part = lax.dynamic_slice_in_dim(segment_all, offset, width_rows, 0)
        return attend_block(
            state, key_part, value_part, segment_part, offset, query_heads, query_places, segment_ids
        )

    row_peak, row_total, weighted = lax.fori_loop(0, blocks, turn, initial)
    mixed = weighted / row_total[..., None]
    mixed = jnp.transpose(mixed, (2, 0, 1, 3)).reshape(row_count, heads_here * GROUP * HEAD_DIM)
    return mixed.astype(jnp.bfloat16)


def per_device(parts, queries, keys, values, segment_ids):
    rows = queries.shape[0]
    tokens = rows * parts
    prompt, chain = tokens // 4, tokens // 8
    if parts == 4 and prompt == rows and 2 * chain == rows and rows % ROWS == 0 and keys.shape[1] >= chain:
        return prompt_block_path(queries, keys, values, segment_ids)
    return gathered_path(queries, keys, values, segment_ids)


def solution(mesh):
    placed = (
        P(("groups", "ctx"), ("tp", "sub")),
        P(("groups", "ctx"), ("tp", "sub")),
        P(("groups", "ctx"), ("tp", "sub")),
        P(("groups", "ctx")),
    )
    return jax.shard_map(
        functools.partial(per_device, mesh.shape["ctx"]),
        mesh=mesh,
        in_specs=placed,
        out_specs=P(("groups", "ctx"), ("tp", "sub")),
        check_vma=False,
    )
```

```python
import functools

import jax
import jax.numpy as jnp
from jax import lax
from jax.experimental import pallas as pl
from jax.experimental.pallas import tpu as pltpu
from jax.sharding import PartitionSpec as P

HEAD_DIM = 128
GROUP = 8
LANES = 128
ROWS = 128
NEG = -1e30
EXP2_SCALE = 1.4426950408889634 * HEAD_DIM ** (-0.5)

VMEM = pl.BlockSpec(memory_space=pltpu.VMEM)
SMEM = pl.BlockSpec(memory_space=pltpu.SMEM)
HBM = pl.BlockSpec(memory_space=pltpu.HBM)


def dot_t(a, b):
    return lax.dot_general(a, b, (((1,), (1,)), ((), ())), preferred_element_type=jnp.float32)


def head_cols(kv_head):
    first = kv_head * GROUP * HEAD_DIM
    return [slice(first + g * HEAD_DIM, first + (g + 1) * HEAD_DIM) for g in range(GROUP)]


def shifted(cols, by):
    return [slice(c.start + by, c.stop + by) for c in cols]


def stack(ref, rows, cols):
    return jnp.concatenate([ref[rows, c] for c in cols], axis=0)


def unstack(ref, rows, cols, value):
    for g, c in enumerate(cols):
        ref[rows, c] = value[g * ROWS : (g + 1) * ROWS].astype(ref.dtype)


def widen(lane_copies, width):
    whole = -(-width // LANES)
    return jnp.concatenate([lane_copies] * whole, axis=1)[:, :width]


def with_ones(wide, source, rows, heads):
    for h in range(heads):
        wide[0:rows, 2 * h * HEAD_DIM : (2 * h + 1) * HEAD_DIM] = source[0:rows, h * HEAD_DIM : (h + 1) * HEAD_DIM]


def fill_ones(wide, heads):
    for h in range(heads):
        wide[:, (2 * h + 1) * HEAD_DIM : (2 * h + 2) * HEAD_DIM] = jnp.ones((wide.shape[0], HEAD_DIM), jnp.bfloat16)


def fetch(source, target, sem):
    copy = pltpu.make_async_copy(source, target, sem)
    copy.start()
    return copy


def pack_kernel(place_ref, k_hbm, v_hbm, seg_hbm, mixed_ref, seg_ref, sem):
    count = k_hbm.shape[0]
    half = count // 2
    place = place_ref[0]
    low, high = pl.ds(0, half), pl.ds(half, half)
    get_seg = fetch(seg_hbm, seg_ref, sem.at[2])

    @pl.when(place == 0)
    def _():
        fetch(v_hbm.at[low], mixed_ref.at[low], sem.at[0])

    @pl.when(place > 0)
    def _():
        fetch(k_hbm.at[high], mixed_ref.at[low], sem.at[0])

    other = fetch(v_hbm.at[high], mixed_ref.at[high], sem.at[1])
    get_seg.wait()
    seg = seg_ref[...].reshape(1, count).astype(jnp.float32)[:, half:]
    pltpu.make_async_copy(k_hbm.at[high], mixed_ref.at[low], sem.at[0]).wait()

    @pl.when(place > 0)
    def _():
        first = lax.broadcasted_iota(jnp.int32, (16, half), 0) == 0
        old = mixed_ref[0:16, 0:half].astype(jnp.float32)
        mixed_ref[0:16, 0:half] = jnp.where(first, jnp.broadcast_to(seg, (16, half)), old).astype(jnp.bfloat16)

    other.wait()


def own_kernel(q_hbm, k_hbm, v_hbm, seg_hbm, state, q_ref, k_ref, v_ref, seg_ref, bias, wide, in_sem):
    count, width = q_ref.shape
    heads = k_ref.shape[1] // HEAD_DIM
    blocks = count // ROWS
    span = [slice(b * ROWS, (b + 1) * ROWS) for b in range(blocks)]
    get_seg = fetch(seg_hbm, seg_ref, in_sem.at[blocks + 2])
    get_k = fetch(k_hbm, k_ref, in_sem.at[blocks])
    get_q = [fetch(q_hbm.at[rows], q_ref.at[rows], in_sem.at[b]) for b, rows in enumerate(span)]
    get_v = fetch(v_hbm, v_ref, in_sem.at[blocks + 1])
    get_seg.wait()
    seg = seg_ref[...].reshape(1, count).astype(jnp.float32)
    for b in range(blocks):
        of_row = jnp.broadcast_to(seg[:, span[b]], (ROWS, ROWS)).T
        for t in range(b + 1):
            of_key = jnp.broadcast_to(seg[:, span[t]], (ROWS, ROWS))
            seen = (of_key == of_row) | (of_key == 0.0)
            if t == b:
                i = lax.broadcasted_iota(jnp.int32, (ROWS, ROWS), 0)
                j = lax.broadcasted_iota(jnp.int32, (ROWS, ROWS), 1)
                seen = seen & (j <= i)
            bias[span[b], span[t]] = jnp.where(seen, 0.0, NEG)
    fill_ones(wide, heads)
    get_k.wait()
    get_v.wait()
    with_ones(wide, v_ref, count, heads)
    lane = lax.broadcasted_iota(jnp.int32, (ROWS, LANES), 1)
    for b in range(blocks):
        rows, keys = span[b], (b + 1) * ROWS
        get_q[b].wait()
        peaks = jnp.zeros((ROWS, LANES), jnp.float32)
        totals = jnp.ones((ROWS, LANES), jnp.float32)
        for h in range(heads):
            cols = head_cols(h)
            scores = dot_t(stack(q_ref, rows, cols), k_ref[0:keys, h * HEAD_DIM : (h + 1) * HEAD_DIM])
            scores = scores.reshape(GROUP, ROWS, keys) + bias[rows, 0:keys][None]
            peak = jnp.max(scores, axis=-1, keepdims=True)
            weights = jnp.exp2((scores - peak) * EXP2_SCALE).astype(jnp.bfloat16).reshape(GROUP * ROWS, keys)
            sums = jnp.dot(
                weights, wide[0:keys, 2 * h * HEAD_DIM : (2 * h + 2) * HEAD_DIM], preferred_element_type=jnp.float32
            )
            unstack(state, rows, cols, sums[:, :HEAD_DIM] / sums[:, HEAD_DIM:])
            for g in range(GROUP):
                here = lane == h * GROUP + g
                peaks = jnp.where(here, peak[g], peaks)
                totals = jnp.where(here, sums[g * ROWS : (g + 1) * ROWS, HEAD_DIM:], totals)
        state[rows, width : width + LANES] = peaks
        state[rows, width + LANES : width + 2 * LANES] = totals


def scores_kernel(here, place_ref, q_ref, k_ref, w_ref, peak_ref):
    count = q_ref.shape[0]
    heads = k_ref.shape[1] // HEAD_DIM

    @pl.when(place_ref[0] == here)
    def _():
        lane = lax.broadcasted_iota(jnp.int32, (ROWS, LANES), 1)
        for b in range(count // ROWS):
            rows = slice(b * ROWS, (b + 1) * ROWS)
            peaks = jnp.zeros((ROWS, LANES), jnp.float32)
            for h in range(heads):
                cols = head_cols(h)
                scores = dot_t(stack(q_ref, rows, cols), k_ref[:, h * HEAD_DIM : (h + 1) * HEAD_DIM])
                peak = jnp.max(scores, axis=-1, keepdims=True)
                weights = jnp.exp2((scores - peak) * EXP2_SCALE).astype(jnp.bfloat16)
                first = (h * (count // ROWS) + b) * GROUP * ROWS
                w_ref[first : first + GROUP * ROWS, :] = weights
                for g in range(GROUP):
                    peaks = jnp.where(lane == h * GROUP + g, peak[g * ROWS : (g + 1) * ROWS], peaks)
            peak_ref[rows, :] = peaks


def column(stats, index):
    return jnp.broadcast_to(stats[:, index : index + 1], (stats.shape[0], LANES))


def merge_tail(q_ref, t_ref, seg_ref, peaks_of, tail, wide, finish):
    count, width = q_ref.shape
    heads = width // HEAD_DIM // GROUP
    half = count // 2
    padded = tail.shape[0]
    pad = padded - half
    fill_ones(wide, heads)
    for h in range(heads):
        mine = slice(h * HEAD_DIM, (h + 1) * HEAD_DIM)
        tail[0:pad, mine] = jnp.zeros((pad, HEAD_DIM), jnp.bfloat16)
        tail[pad:padded, mine] = t_ref[0:half, mine]
        wide[0:pad, 2 * h * HEAD_DIM : (2 * h + 1) * HEAD_DIM] = jnp.zeros((pad, HEAD_DIM), jnp.bfloat16)
        wide[pad:padded, 2 * h * HEAD_DIM : (2 * h + 1) * HEAD_DIM] = t_ref[half : 2 * half, mine]
    of_keys = t_ref[0:16, 0:half].astype(jnp.float32)[0:1]
    of_keys = jnp.concatenate([jnp.full((1, pad), -1.0, jnp.float32), of_keys], axis=1)
    of_keys = jnp.where(lax.broadcasted_iota(jnp.int32, (1, padded), 1) <= pad, -1.0, of_keys)
    seg = seg_ref[...].reshape(1, count).astype(jnp.float32)
    for start in range(0, half, ROWS):
        size = min(ROWS, half - start)
        low = (start + pad) // LANES * LANES
        keys = padded - low
        rows = slice(start, start + size)
        of_row = jnp.broadcast_to(seg[:, start : start + ROWS], (ROWS, ROWS)).T[0:size]
        seen = widen(of_row, keys) == jnp.broadcast_to(of_keys[:, low:], (size, keys))
        bias = jnp.where(seen, 0.0, NEG)
        for h in range(heads):
            cols = head_cols(h)
            queries = jnp.concatenate([q_ref[rows, c] for c in cols], axis=0)
            scores = dot_t(queries, tail[low:padded, h * HEAD_DIM : (h + 1) * HEAD_DIM])
            scores = (scores.reshape(GROUP, size, keys) + bias[None]).reshape(GROUP * size, keys)
            own = peaks_of(rows, h)
            peak = jnp.maximum(own, jnp.max(scores, axis=-1, keepdims=True))
            weights = jnp.exp2((scores - widen(peak, keys)) * EXP2_SCALE).astype(jnp.bfloat16)
            sums = jnp.dot(
                weights, wide[low:padded, 2 * h * HEAD_DIM : (2 * h + 2) * HEAD_DIM], preferred_element_type=jnp.float32
            )
            scale = jnp.exp2((own - peak) * EXP2_SCALE)
            finish(rows, h, cols, peak, scale, sums)


def tail_kernel(place_ref, q_ref, t_ref, seg_ref, state_in, state, tail, wide):
    width = q_ref.shape[1]

    def peaks_of(rows, h):
        peaks = state_in[rows, width : width + LANES]
        return jnp.concatenate([column(peaks, h * GROUP + g) for g in range(GROUP)], axis=0)

    def finish(rows, h, cols, peak, scale, sums):
        size = rows.stop - rows.start
        lane = lax.broadcasted_iota(jnp.int32, (size, LANES), 1)
        old_totals = state_in[rows, width + LANES : width + 2 * LANES]
        peaks = state[rows, width : width + LANES]
        totals = state[rows, width + LANES : width + 2 * LANES]
        for g, c in enumerate(cols):
            mine = slice(g * size, (g + 1) * size)
            index = h * GROUP + g
            old = column(old_totals, index) * scale[mine]
            total = old + sums[mine, HEAD_DIM:]
            state[rows, c] = (state[rows, c] * old + sums[mine, :HEAD_DIM]) / total
            peaks = jnp.where(lane == index, peak[mine], peaks)
            totals = jnp.where(lane == index, total, totals)
        state[rows, width : width + LANES] = peaks
        state[rows, width + LANES : width + 2 * LANES] = totals

    @pl.when(place_ref[0] == 3)
    def _():
        merge_tail(q_ref, t_ref, seg_ref, peaks_of, tail, wide, finish)


def put_out(staged, out_ref, sem, rows, h, waits):
    box = (pl.ds(rows.start, rows.stop - rows.start), pl.ds(h * GROUP * HEAD_DIM, GROUP * HEAD_DIM))
    waits.append(fetch(staged.at[box], out_ref.at[box], sem.at[rows.start // ROWS, h]))


def prompt_blocks(w_ref, v_ref, state, ppeak_ref, wide, finish):
    count = v_ref.shape[0]
    heads = v_ref.shape[1] // HEAD_DIM
    width = heads * GROUP * HEAD_DIM
    fill_ones(wide, heads)
    with_ones(wide, v_ref, count, heads)
    for b in range(count // ROWS):
        rows = slice(b * ROWS, (b + 1) * ROWS)
        own, prompt = state[rows, width : width + LANES], ppeak_ref[rows, :]
        peak = jnp.maximum(own, prompt)
        prompt_scale = jnp.exp2((prompt - peak) * EXP2_SCALE)
        own_total = state[rows, width + LANES : width + 2 * LANES] * jnp.exp2((own - peak) * EXP2_SCALE)
        for h in range(heads):
            first = (h * (count // ROWS) + b) * GROUP * ROWS
            sums = jnp.dot(
                w_ref[first : first + GROUP * ROWS, :],
                wide[:, 2 * h * HEAD_DIM : (2 * h + 2) * HEAD_DIM],
                preferred_element_type=jnp.float32,
            )
            for g, c in enumerate(head_cols(h)):
                index = h * GROUP + g
                mine = slice(g * ROWS, (g + 1) * ROWS)
                own_part, prompt_part = column(own_total, index), column(prompt_scale, index)
                total = own_part + sums[mine, HEAD_DIM:] * prompt_part
                value = (state[rows, c] * own_part + sums[mine, :HEAD_DIM] * prompt_part) / total
                finish(rows, h, g, c, value, peak, total)


def prompt_kernel(here, place_ref, w_ref, v_ref, state, ppeak_ref, *rest):
    out_ref, wide, staged, sem = rest[-4:]
    count, width = staged.shape
    heads = width // HEAD_DIM // GROUP

    if here == 1:

        @pl.when(place_ref[0] == 0)
        def _():
            waits = []
            for b in range(count // ROWS):
                rows = slice(b * ROWS, (b + 1) * ROWS)
                for h in range(heads):
                    for c in head_cols(h):
                        staged[rows, c] = state[rows, c].astype(jnp.bfloat16)
                    put_out(staged, out_ref, sem, rows, h, waits)
            for wait in waits:
                wait.wait()

    @pl.when(place_ref[0] == here)
    def _():
        waits = []

        def finish(rows, h, g, c, value, peak, total):
            staged[rows, c] = value.astype(jnp.bfloat16)
            if g == GROUP - 1:
                put_out(staged, out_ref, sem, rows, h, waits)

        prompt_blocks(w_ref, v_ref, state, ppeak_ref, wide, finish)
        for wait in waits:
            wait.wait()


def prompt_first_kernel(place_ref, w_ref, v_ref, state, ppeak_ref, out_ref, aux, wide, staged, sem):
    width = staged.shape[1]

    @pl.when(place_ref[0] == 2)
    def _():
        waits = []

        def finish(rows, h, g, c, value, peak, total):
            if rows.stop <= aux.shape[0]:
                peak_cols, sum_cols = shifted([c], width)[0], shifted([c], 2 * width)[0]
                aux[rows, c] = value
                aux[rows, peak_cols] = column(peak, h * GROUP + g)
                aux[rows, sum_cols] = total
            else:
                staged[rows, c] = value.astype(jnp.bfloat16)
                if g == GROUP - 1:
                    put_out(staged, out_ref, sem, rows, h, waits)

        prompt_blocks(w_ref, v_ref, state, ppeak_ref, wide, finish)
        for wait in waits:
            wait.wait()


def last_kernel(place_ref, q_ref, t_ref, seg_ref, aux, out_in, out_ref, tail, wide, staged, sem):
    count, width = q_ref.shape
    heads = width // HEAD_DIM // GROUP
    half = count // 2

    @pl.when(place_ref[0] == 2)
    def _():
        waits = []

        def peaks_of(rows, h):
            return stack(aux, rows, shifted(head_cols(h), width))

        def finish(rows, h, cols, peak, scale, sums):
            size = rows.stop - rows.start
            for g, c in enumerate(cols):
                mine = slice(g * size, (g + 1) * size)
                total = aux[rows, shifted([c], 2 * width)[0]] * scale[mine]
                value = (aux[rows, c] * total + sums[mine, :HEAD_DIM]) / (total + sums[mine, HEAD_DIM:])
                staged[rows, c] = value.astype(jnp.bfloat16)
            put_out(staged, out_ref, sem, rows, h, waits)

        if aux.shape[0] > half:
            rest = slice(half, aux.shape[0])
            staged[rest, :] = aux[rest, 0:width].astype(jnp.bfloat16)
            box = (pl.ds(half, aux.shape[0] - half), pl.ds(0, width))
            waits.append(fetch(staged.at[box], out_ref.at[box], sem.at[count // ROWS, 0]))
        merge_tail(q_ref, t_ref, seg_ref, peaks_of, tail, wide, finish)
        for wait in waits:
            wait.wait()


def params(mebibytes):
    return pltpu.CompilerParams(vmem_limit_bytes=mebibytes << 20)


def cost(flops):
    return pl.CostEstimate(flops=flops, bytes_accessed=1, transcendentals=0)


def prompt_block_path(queries, keys, values, segment_ids):
    count, kv_width = keys.shape
    width = queries.shape[1]
    half = count // 2
    padded = -(-half // LANES) * LANES
    blocks = count // ROWS
    place = lax.axis_index("ctx").astype(jnp.int32).reshape(1)
    in_hbm = [pltpu.with_memory_space_constraint(x, pltpu.HBM) for x in (queries, keys, values, segment_ids)]

    keys_2 = lax.ppermute(keys, "ctx", [(0, 2)])
    mixed_shape = jax.ShapeDtypeStruct(keys.shape, jnp.bfloat16)
    mixed = pl.pallas_call(
        pack_kernel,
        out_shape=mixed_shape,
        in_specs=[SMEM] + [HBM] * 3,
        out_specs=VMEM,
        scratch_shapes=[pltpu.VMEM(segment_ids.shape, jnp.int32), pltpu.SemaphoreType.DMA((3,))],
        compiler_params=params(2),
        cost_estimate=cost(1),
        name="pack",
    )(place, *in_hbm[1:])
    two_left = lax.ppermute(mixed, "ctx", [(0, 2), (2, 3)])

    state_shape = jax.ShapeDtypeStruct((count, width + 2 * LANES), jnp.float32)
    state = pl.pallas_call(
        own_kernel,
        out_shape=state_shape,
        in_specs=[HBM] * 4,
        out_specs=VMEM,
        scratch_shapes=[
            pltpu.VMEM(queries.shape, jnp.bfloat16),
            pltpu.VMEM(keys.shape, jnp.bfloat16),
            pltpu.VMEM(keys.shape, jnp.bfloat16),
            pltpu.VMEM(segment_ids.shape, jnp.int32),
            pltpu.VMEM((count, count), jnp.float32),
            pltpu.VMEM((count, 2 * kv_width), jnp.bfloat16),
            pltpu.SemaphoreType.DMA((blocks + 3,)),
        ],
        compiler_params=params(10),
        cost_estimate=cost(16 * count * count * width),
        name="own",
    )(*in_hbm)

    keys_2, mixed, state = lax.optimization_barrier((keys_2, mixed, state))
    keys_3 = lax.ppermute(keys_2, "ctx", [(2, 3)])
    keys_1 = lax.ppermute(keys_2, "ctx", [(2, 1)])
    values_1 = lax.ppermute(mixed, "ctx", [(0, 1)])
    tail_2 = lax.ppermute(mixed, "ctx", [(1, 2)])
    values_3 = lax.ppermute(two_left, "ctx", [(2, 3)])

    tail_scratch = [pltpu.VMEM((padded, kv_width), jnp.bfloat16), pltpu.VMEM((padded, 2 * kv_width), jnp.bfloat16)]
    state = pl.pallas_call(
        tail_kernel,
        out_shape=state_shape,
        in_specs=[SMEM] + [VMEM] * 4,
        out_specs=VMEM,
        scratch_shapes=tail_scratch,
        input_output_aliases={4: 0},
        compiler_params=params(8),
        cost_estimate=cost(1),
        name="tail",
    )(place, queries, two_left, segment_ids, state)

    stats = jax.ShapeDtypeStruct((count, LANES), jnp.float32)
    weights_shape = jax.ShapeDtypeStruct((count * width // HEAD_DIM, count), jnp.bfloat16)

    def scores(here, key_block):
        return pl.pallas_call(
            functools.partial(scores_kernel, here),
            out_shape=(weights_shape, stats),
            in_specs=[SMEM] + [VMEM] * 2,
            out_specs=(VMEM,) * 2,
            compiler_params=params(8),
            cost_estimate=cost(8 * count * count * width),
            name=f"scores_{here}",
        )(place, queries, key_block)

    out_shape = jax.ShapeDtypeStruct(queries.shape, jnp.bfloat16)
    reached = -(-half // ROWS) * ROWS
    aux_shape = jax.ShapeDtypeStruct((reached, 3 * width), jnp.float32)
    out_scratch = [
        pltpu.VMEM((count, 2 * kv_width), jnp.bfloat16),
        pltpu.VMEM(queries.shape, jnp.bfloat16),
        pltpu.SemaphoreType.DMA((blocks, kv_width // HEAD_DIM)),
    ]
    weights, prompt_peak = scores(2, keys_2)
    out, aux = pl.pallas_call(
        prompt_first_kernel,
        out_shape=(out_shape, aux_shape),
        in_specs=[SMEM] + [VMEM] * 4,
        out_specs=(HBM, VMEM),
        scratch_shapes=out_scratch,
        compiler_params=params(8),
        cost_estimate=cost(1),
        name="prompt_2",
    )(place, weights, two_left, state, prompt_peak)
    for here, key_block, value_block in ((3, keys_3, values_3), (1, keys_1, values_1)):
        weights, prompt_peak = scores(here, key_block)
        out = pl.pallas_call(
            functools.partial(prompt_kernel, here),
            out_shape=out_shape,
            in_specs=[SMEM] + [VMEM] * 4 + [HBM],
            out_specs=HBM,
            scratch_shapes=out_scratch,
            input_output_aliases={5: 0},
            compiler_params=params(8),
            cost_estimate=cost(1),
            name=f"prompt_{here}",
        )(place, weights, value_block, state, prompt_peak, out)

    return pl.pallas_call(
        last_kernel,
        out_shape=out_shape,
        in_specs=[SMEM] + [VMEM] * 4 + [HBM],
        out_specs=HBM,
        scratch_shapes=tail_scratch
        + [pltpu.VMEM((reached, width), jnp.bfloat16), pltpu.SemaphoreType.DMA((blocks + 1, kv_width // HEAD_DIM))],
        input_output_aliases={5: 0},
        compiler_params=params(8),
        cost_estimate=cost(1),
        name="last",
    )(place, queries, tail_2, segment_ids, aux, out)


def attend_block(
    running,
    key_block,
    value_block,
    segment_block,
    first_row,
    query_heads,
    query_places,
    query_segment,
):
    number = key_block.shape[0]
    heads_here = key_block.shape[1] // HEAD_DIM
    key_places = first_row + jnp.arange(number, dtype=jnp.int32)
    same = (segment_block[None, :] == query_segment[:, None]) | (segment_block[None, :] == 0)
    visible = (key_places[None, :] <= query_places[:, None]) & same
    key_heads = key_block.reshape(number, heads_here, HEAD_DIM)
    value_heads = value_block.reshape(number, heads_here, HEAD_DIM)

    def compute(state):
        row_peak, row_total, weighted = state
        scores = jnp.einsum(
            "qhgd,khd->hgqk", query_heads, key_heads, preferred_element_type=jnp.float32
        ) * HEAD_DIM ** (-0.5)
        scores = jnp.where(visible[None, None], scores, -1e30)
        new_peak = jnp.maximum(row_peak, jnp.max(scores, axis=-1))
        factor = jnp.exp(row_peak - new_peak)
        weights = jnp.where(visible[None, None], jnp.exp(scores - new_peak[..., None]), 0.0)
        new_total = row_total * factor + jnp.sum(weights, axis=-1)
        added = jnp.einsum(
            "hgqk,khd->hgqd",
            weights.astype(jnp.bfloat16),
            value_heads,
            preferred_element_type=jnp.float32,
        )
        return (new_peak, new_total, weighted * factor[..., None] + added)

    return lax.cond(jnp.any(visible), compute, lambda state: state, running)


def gathered_path(queries, keys, values, segment_ids):
    row_count = queries.shape[0]
    heads_here = keys.shape[1] // HEAD_DIM
    my_index = lax.axis_index("ctx")
    query_places = my_index * row_count + jnp.arange(row_count, dtype=jnp.int32)
    query_heads = queries.reshape(row_count, heads_here, GROUP, HEAD_DIM)
    initial = (
        jnp.full((heads_here, GROUP, row_count), -1e30, jnp.float32),
        jnp.zeros((heads_here, GROUP, row_count), jnp.float32),
        jnp.zeros((heads_here, GROUP, row_count, HEAD_DIM), jnp.float32),
    )
    key_all = lax.all_gather(keys, "ctx", axis=0, tiled=True)
    value_all = lax.all_gather(values, "ctx", axis=0, tiled=True)
    segment_all = lax.all_gather(segment_ids, "ctx", axis=0, tiled=True)
    blocks = max(1, key_all.shape[0] // row_count)
    width_rows = key_all.shape[0] // blocks

    def turn(number, state):
        offset = number * width_rows
        key_part = lax.dynamic_slice_in_dim(key_all, offset, width_rows, 0)
        value_part = lax.dynamic_slice_in_dim(value_all, offset, width_rows, 0)
        segment_part = lax.dynamic_slice_in_dim(segment_all, offset, width_rows, 0)
        return attend_block(
            state, key_part, value_part, segment_part, offset, query_heads, query_places, segment_ids
        )

    row_peak, row_total, weighted = lax.fori_loop(0, blocks, turn, initial)
    mixed = weighted / row_total[..., None]
    mixed = jnp.transpose(mixed, (2, 0, 1, 3)).reshape(row_count, heads_here * GROUP * HEAD_DIM)
    return mixed.astype(jnp.bfloat16)


def per_device(parts, queries, keys, values, segment_ids):
    rows = queries.shape[0]
    tokens = rows * parts
    prompt, chain = tokens // 4, tokens // 8
    if parts == 4 and prompt == rows and 2 * chain == rows and rows % ROWS == 0 and keys.shape[1] >= chain:
        return prompt_block_path(queries, keys, values, segment_ids)
    return gathered_path(queries, keys, values, segment_ids)


def solution(mesh):
    placed = (
        P(("groups", "ctx"), ("tp", "sub")),
        P(("groups", "ctx"), ("tp", "sub")),
        P(("groups", "ctx"), ("tp", "sub")),
        P(("groups", "ctx")),
    )
    return jax.shard_map(
        functools.partial(per_device, mesh.shape["ctx"]),
        mesh=mesh,
        in_specs=placed,
        out_specs=P(("groups", "ctx"), ("tp", "sub")),
        check_vma=False,
    )
```

```python
import functools

import jax
import jax.numpy as jnp
from jax import lax
from jax.experimental import pallas as pl
from jax.experimental.pallas import tpu as pltpu
from jax.sharding import PartitionSpec as P

HEAD_DIM = 128
GROUP = 8
LANES = 128
ROWS = 128
NEG = -1e30
EXP2_SCALE = 1.4426950408889634 * HEAD_DIM ** (-0.5)

VMEM = pl.BlockSpec(memory_space=pltpu.VMEM)
SMEM = pl.BlockSpec(memory_space=pltpu.SMEM)
HBM = pl.BlockSpec(memory_space=pltpu.HBM)


def dot_t(a, b):
    return lax.dot_general(a, b, (((1,), (1,)), ((), ())), preferred_element_type=jnp.float32)


def head_cols(kv_head):
    first = kv_head * GROUP * HEAD_DIM
    return [slice(first + g * HEAD_DIM, first + (g + 1) * HEAD_DIM) for g in range(GROUP)]


def shifted(cols, by):
    return [slice(c.start + by, c.stop + by) for c in cols]


def stack(ref, rows, cols):
    return jnp.concatenate([ref[rows, c] for c in cols], axis=0)


def unstack(ref, rows, cols, value):
    for g, c in enumerate(cols):
        ref[rows, c] = value[g * ROWS : (g + 1) * ROWS].astype(ref.dtype)


def widen(lane_copies, width):
    whole = -(-width // LANES)
    return jnp.concatenate([lane_copies] * whole, axis=1)[:, :width]


def with_ones(wide, source, rows, heads):
    for h in range(heads):
        wide[0:rows, 2 * h * HEAD_DIM : (2 * h + 1) * HEAD_DIM] = source[0:rows, h * HEAD_DIM : (h + 1) * HEAD_DIM]


def fill_ones(wide, heads):
    for h in range(heads):
        wide[:, (2 * h + 1) * HEAD_DIM : (2 * h + 2) * HEAD_DIM] = jnp.ones((wide.shape[0], HEAD_DIM), jnp.bfloat16)


def fetch(source, target, sem):
    copy = pltpu.make_async_copy(source, target, sem)
    copy.start()
    return copy


def pack_kernel(place_ref, q_hbm, k_hbm, v_hbm, seg_hbm, mixed_ref, state, seg_ref, sem, *own_scratch):
    count = k_hbm.shape[0]
    half = count // 2
    place = place_ref[0]
    low, high = pl.ds(0, half), pl.ds(half, half)

    @pl.when(place == 0)
    def _():
        every = fetch(v_hbm, mixed_ref, sem.at[0])
        get_seg = fetch(seg_hbm, seg_ref, sem.at[2])
        attend_own(0, 1, get_seg, q_hbm, k_hbm, v_hbm, state, seg_ref, *own_scratch)
        every.wait()

    @pl.when((place > 0) & (place < 3))
    def _():
        get_seg = fetch(seg_hbm, seg_ref, sem.at[2])
        first = fetch(k_hbm.at[high], mixed_ref.at[low], sem.at[0])
        other = fetch(v_hbm.at[high], mixed_ref.at[high], sem.at[1])
        get_seg.wait()
        seg = seg_ref[...].reshape(1, count).astype(jnp.float32)[:, half:]
        first.wait()
        top = lax.broadcasted_iota(jnp.int32, (16, half), 0) == 0
        old = mixed_ref[0:16, 0:half].astype(jnp.float32)
        mixed_ref[0:16, 0:half] = jnp.where(top, jnp.broadcast_to(seg, (16, half)), old).astype(jnp.bfloat16)
        other.wait()


def attend_own(
    first_head, heads, get_seg, q_hbm, k_hbm, v_hbm, state, seg_ref, q_ref, k_ref, v_ref, bias, wide, in_sem
):
    count, width = q_ref.shape
    blocks = count // ROWS
    span = [slice(b * ROWS, (b + 1) * ROWS) for b in range(blocks)]
    here = slice(first_head * GROUP * HEAD_DIM, (first_head + heads) * GROUP * HEAD_DIM)
    get_k = fetch(k_hbm, k_ref, in_sem.at[blocks])
    get_q = [fetch(q_hbm.at[rows, here], q_ref.at[rows, here], in_sem.at[b]) for b, rows in enumerate(span)]
    get_v = fetch(v_hbm, v_ref, in_sem.at[blocks + 1])
    get_seg.wait()
    seg = seg_ref[...].reshape(1, count).astype(jnp.float32)
    for b in range(blocks):
        of_row = jnp.broadcast_to(seg[:, span[b]], (ROWS, ROWS)).T
        for t in range(b + 1):
            of_key = jnp.broadcast_to(seg[:, span[t]], (ROWS, ROWS))
            seen = (of_key == of_row) | (of_key == 0.0)
            if t == b:
                i = lax.broadcasted_iota(jnp.int32, (ROWS, ROWS), 0)
                j = lax.broadcasted_iota(jnp.int32, (ROWS, ROWS), 1)
                seen = seen & (j <= i)
            bias[span[b], span[t]] = jnp.where(seen, 0.0, NEG)
    fill_ones(wide, k_ref.shape[1] // HEAD_DIM)
    get_k.wait()
    get_v.wait()
    with_ones(wide, v_ref, count, k_ref.shape[1] // HEAD_DIM)
    lane = lax.broadcasted_iota(jnp.int32, (ROWS, LANES), 1)
    for b in range(blocks):
        rows, keys = span[b], (b + 1) * ROWS
        get_q[b].wait()
        if first_head == 0:
            peaks = jnp.zeros((ROWS, LANES), jnp.float32)
            totals = jnp.ones((ROWS, LANES), jnp.float32)
        else:
            peaks = state[rows, width : width + LANES]
            totals = state[rows, width + LANES : width + 2 * LANES]
        for h in range(first_head, first_head + heads):
            cols = head_cols(h)
            scores = dot_t(stack(q_ref, rows, cols), k_ref[0:keys, h * HEAD_DIM : (h + 1) * HEAD_DIM])
            scores = scores.reshape(GROUP, ROWS, keys) + bias[rows, 0:keys][None]
            peak = jnp.max(scores, axis=-1, keepdims=True)
            weights = jnp.exp2((scores - peak) * EXP2_SCALE).astype(jnp.bfloat16).reshape(GROUP * ROWS, keys)
            sums = jnp.dot(
                weights, wide[0:keys, 2 * h * HEAD_DIM : (2 * h + 2) * HEAD_DIM], preferred_element_type=jnp.float32
            )
            unstack(state, rows, cols, sums[:, :HEAD_DIM] / sums[:, HEAD_DIM:])
            for g in range(GROUP):
                mine = lane == h * GROUP + g
                peaks = jnp.where(mine, peak[g], peaks)
                totals = jnp.where(mine, sums[g * ROWS : (g + 1) * ROWS, HEAD_DIM:], totals)
        state[rows, width : width + LANES] = peaks
        state[rows, width + LANES : width + 2 * LANES] = totals


def own_kernel(place_ref, q_hbm, k_hbm, v_hbm, seg_hbm, state_in, state, seg_ref, *scratch):
    heads = k_hbm.shape[1] // HEAD_DIM
    get_seg = fetch(seg_hbm, seg_ref, scratch[-1].at[k_hbm.shape[0] // ROWS + 2])

    @pl.when(place_ref[0] > 0)
    def _():
        attend_own(0, heads, get_seg, q_hbm, k_hbm, v_hbm, state, seg_ref, *scratch)

    @pl.when(place_ref[0] == 0)
    def _():
        attend_own(1, heads - 1, get_seg, q_hbm, k_hbm, v_hbm, state, seg_ref, *scratch)


def scores_kernel(places, place_ref, q_ref, *refs):
    *k_refs, w_ref, peak_ref, k_ref = refs
    count = q_ref.shape[0]
    heads = k_ref.shape[1] // HEAD_DIM
    lane = lax.broadcasted_iota(jnp.int32, (ROWS, LANES), 1)

    place = place_ref[0]

    for here, ref in zip(places, k_refs):

        @pl.when(place == here)
        def _(ref=ref):
            k_ref[...] = ref[...]

    @pl.when(functools.reduce(jnp.logical_or, [place == here for here in places]))
    def _():
        for b in range(count // ROWS):
            rows = slice(b * ROWS, (b + 1) * ROWS)
            peaks = jnp.zeros((ROWS, LANES), jnp.float32)
            for h in range(heads):
                cols = head_cols(h)
                scores = dot_t(stack(q_ref, rows, cols), k_ref[:, h * HEAD_DIM : (h + 1) * HEAD_DIM])
                peak = jnp.max(scores, axis=-1, keepdims=True)
                weights = jnp.exp2((scores - peak) * EXP2_SCALE).astype(jnp.bfloat16)
                first = (h * (count // ROWS) + b) * GROUP * ROWS
                w_ref[first : first + GROUP * ROWS, :] = weights
                for g in range(GROUP):
                    peaks = jnp.where(lane == h * GROUP + g, peak[g * ROWS : (g + 1) * ROWS], peaks)
            peak_ref[rows, :] = peaks


def column(stats, index):
    return jnp.broadcast_to(stats[:, index : index + 1], (stats.shape[0], LANES))


def merge_tail(q_ref, t_ref, seg_ref, peaks_of, tail, wide, finish):
    count, width = q_ref.shape
    heads = width // HEAD_DIM // GROUP
    half = count // 2
    padded = tail.shape[0]
    pad = padded - half
    fill_ones(wide, heads)
    for h in range(heads):
        mine = slice(h * HEAD_DIM, (h + 1) * HEAD_DIM)
        tail[0:pad, mine] = jnp.zeros((pad, HEAD_DIM), jnp.bfloat16)
        tail[pad:padded, mine] = t_ref[0:half, mine]
        wide[0:pad, 2 * h * HEAD_DIM : (2 * h + 1) * HEAD_DIM] = jnp.zeros((pad, HEAD_DIM), jnp.bfloat16)
        wide[pad:padded, 2 * h * HEAD_DIM : (2 * h + 1) * HEAD_DIM] = t_ref[half : 2 * half, mine]
    of_keys = t_ref[0:16, 0:half].astype(jnp.float32)[0:1]
    of_keys = jnp.concatenate([jnp.full((1, pad), -1.0, jnp.float32), of_keys], axis=1)
    of_keys = jnp.where(lax.broadcasted_iota(jnp.int32, (1, padded), 1) <= pad, -1.0, of_keys)
    seg = seg_ref[...].reshape(1, count).astype(jnp.float32)
    for start in range(0, half, ROWS):
        size = min(ROWS, half - start)
        low = (start + pad) // LANES * LANES
        keys = padded - low
        rows = slice(start, start + size)
        of_row = jnp.broadcast_to(seg[:, start : start + ROWS], (ROWS, ROWS)).T[0:size]
        seen = widen(of_row, keys) == jnp.broadcast_to(of_keys[:, low:], (size, keys))
        bias = jnp.where(seen, 0.0, NEG)
        for h in range(heads):
            cols = head_cols(h)
            queries = jnp.concatenate([q_ref[rows, c] for c in cols], axis=0)
            scores = dot_t(queries, tail[low:padded, h * HEAD_DIM : (h + 1) * HEAD_DIM])
            scores = (scores.reshape(GROUP, size, keys) + bias[None]).reshape(GROUP * size, keys)
            own = peaks_of(rows, h)
            peak = jnp.maximum(own, jnp.max(scores, axis=-1, keepdims=True))
            weights = jnp.exp2((scores - widen(peak, keys)) * EXP2_SCALE).astype(jnp.bfloat16)
            sums = jnp.dot(
                weights, wide[low:padded, 2 * h * HEAD_DIM : (2 * h + 2) * HEAD_DIM], preferred_element_type=jnp.float32
            )
            scale = jnp.exp2((own - peak) * EXP2_SCALE)
            finish(rows, h, cols, peak, scale, sums)


def tail_kernel(place_ref, q_ref, t_ref, seg_ref, state_in, state, tail, wide):
    width = q_ref.shape[1]

    def peaks_of(rows, h):
        peaks = state_in[rows, width : width + LANES]
        return jnp.concatenate([column(peaks, h * GROUP + g) for g in range(GROUP)], axis=0)

    def finish(rows, h, cols, peak, scale, sums):
        size = rows.stop - rows.start
        lane = lax.broadcasted_iota(jnp.int32, (size, LANES), 1)
        old_totals = state_in[rows, width + LANES : width + 2 * LANES]
        peaks = state[rows, width : width + LANES]
        totals = state[rows, width + LANES : width + 2 * LANES]
        for g, c in enumerate(cols):
            mine = slice(g * size, (g + 1) * size)
            index = h * GROUP + g
            old = column(old_totals, index) * scale[mine]
            total = old + sums[mine, HEAD_DIM:]
            state[rows, c] = (state[rows, c] * old + sums[mine, :HEAD_DIM]) / total
            peaks = jnp.where(lane == index, peak[mine], peaks)
            totals = jnp.where(lane == index, total, totals)
        state[rows, width : width + LANES] = peaks
        state[rows, width + LANES : width + 2 * LANES] = totals

    @pl.when(place_ref[0] == 3)
    def _():
        merge_tail(q_ref, t_ref, seg_ref, peaks_of, tail, wide, finish)


def prompt_rows(w_ref, state, ppeak_ref, wide, finish):
    count = wide.shape[0]
    heads = wide.shape[1] // 2 // HEAD_DIM
    width = heads * GROUP * HEAD_DIM
    for b in range(count // ROWS):
        rows = slice(b * ROWS, (b + 1) * ROWS)
        own, prompt = state[rows, width : width + LANES], ppeak_ref[rows, :]
        peak = jnp.maximum(own, prompt)
        prompt_scale = jnp.exp2((prompt - peak) * EXP2_SCALE)
        own_total = state[rows, width + LANES : width + 2 * LANES] * jnp.exp2((own - peak) * EXP2_SCALE)
        for h in range(heads):
            first = (h * (count // ROWS) + b) * GROUP * ROWS
            pieces = 2 if (b, h) == (count // ROWS - 1, heads - 1) else 1
            size = GROUP // pieces
            for p in range(pieces):
                low = first + p * size * ROWS
                sums = jnp.dot(
                    w_ref[low : low + size * ROWS, :],
                    wide[:, 2 * h * HEAD_DIM : (2 * h + 2) * HEAD_DIM],
                    preferred_element_type=jnp.float32,
                )
                cols = head_cols(h)[p * size : (p + 1) * size]
                for g, c in enumerate(cols):
                    index = h * GROUP + p * size + g
                    mine = slice(g * ROWS, (g + 1) * ROWS)
                    own_part, prompt_part = column(own_total, index), column(prompt_scale, index)
                    total = own_part + sums[mine, HEAD_DIM:] * prompt_part
                    value = (state[rows, c] * own_part + sums[mine, :HEAD_DIM] * prompt_part) / total
                    finish(rows, c, value, index, peak, total)
                finish(rows, slice(cols[0].start, cols[-1].stop), None, None, None, None)


def middle_kernel(place_ref, w_ref, v_ref, state, ppeak_ref, out_ref, aux, wide, staged, sem):
    width = staged.shape[1]
    heads = width // HEAD_DIM // GROUP

    @pl.when(place_ref[0] == 2)
    def _():
        waits = []

        def finish(rows, cols, value, index, peak, total):
            goes_on = rows.stop <= aux.shape[0]
            if value is None:
                if not goes_on:
                    put_out(staged, out_ref, sem, rows, cols, waits)
            elif goes_on:
                aux[rows, cols] = value
                aux[rows, shifted([cols], width)[0]] = column(peak, index)
                aux[rows, shifted([cols], 2 * width)[0]] = total
            else:
                staged[rows, cols] = value.astype(jnp.bfloat16)

        fill_ones(wide, heads)
        with_ones(wide, v_ref, staged.shape[0], heads)
        prompt_rows(w_ref, state, ppeak_ref, wide, finish)
        for wait in waits:
            wait.wait()


def put_out(staged, out_ref, sem, rows, cols, waits):
    box = (pl.ds(rows.start, rows.stop - rows.start), pl.ds(cols.start, cols.stop - cols.start))
    waits.append(fetch(staged.at[box], out_ref.at[box], sem.at[len(waits)]))


def last_kernel(
    place_ref, q_ref, w_ref, one_ref, v3_ref, seg_ref, state, ppeak_ref, aux, out_in, out_ref, wide, tail, tail_wide, staged, sem
):
    count, width = q_ref.shape
    heads = width // HEAD_DIM // GROUP
    half = count // 2
    place = place_ref[0]

    def run(body):
        waits = []

        def put(rows, cols):
            put_out(staged, out_ref, sem, rows, cols, waits)

        body(put)
        for wait in waits:
            wait.wait()

    @pl.when(place == 0)
    def _():
        def body(put):
            for b in range(count // ROWS):
                rows = slice(b * ROWS, (b + 1) * ROWS)
                staged[rows, :] = state[rows, 0:width].astype(jnp.bfloat16)
                put(rows, slice(0, width))

        run(body)

    for here, ref in ((1, one_ref), (3, v3_ref)):
        pl.when(place == here)(functools.partial(with_ones, wide, ref, count, heads))

    @pl.when((place == 1) | (place == 3))
    def _():
        fill_ones(wide, heads)

        def body(put):
            def finish(rows, cols, value, index, peak, total):
                if value is None:
                    put(rows, cols)
                else:
                    staged[rows, cols] = value.astype(jnp.bfloat16)

            prompt_rows(w_ref, state, ppeak_ref, wide, finish)

        run(body)

    @pl.when(place == 2)
    def _():
        def body(put):
            def peaks_of(rows, h):
                return stack(aux, rows, shifted(head_cols(h), width))

            def finish(rows, h, cols, peak, scale, sums):
                size = rows.stop - rows.start
                for g, c in enumerate(cols):
                    mine = slice(g * size, (g + 1) * size)
                    total = aux[rows, shifted([c], 2 * width)[0]] * scale[mine]
                    value = (aux[rows, c] * total + sums[mine, :HEAD_DIM]) / (total + sums[mine, HEAD_DIM:])
                    staged[rows, c] = value.astype(jnp.bfloat16)
                put(rows, slice(cols[0].start, cols[-1].stop))

            if aux.shape[0] > half:
                rest = slice(half, aux.shape[0])
                staged[rest, :] = aux[rest, 0:width].astype(jnp.bfloat16)
                put(rest, slice(0, width))
            merge_tail(q_ref, one_ref, seg_ref, peaks_of, tail, tail_wide, finish)

        run(body)


def params(mebibytes):
    return pltpu.CompilerParams(vmem_limit_bytes=mebibytes << 20)


def cost(flops):
    return pl.CostEstimate(flops=flops, bytes_accessed=1, transcendentals=0)


def prompt_block_path(queries, keys, values, segment_ids):
    count, kv_width = keys.shape
    width = queries.shape[1]
    half = count // 2
    padded = -(-half // LANES) * LANES
    blocks = count // ROWS
    place = lax.axis_index("ctx").astype(jnp.int32).reshape(1)
    in_hbm = [pltpu.with_memory_space_constraint(x, pltpu.HBM) for x in (queries, keys, values, segment_ids)]

    keys_2 = lax.ppermute(keys, "ctx", [(0, 2)])
    state_shape = jax.ShapeDtypeStruct((count, width + 2 * LANES), jnp.float32)
    own_scratch = [
        pltpu.VMEM(queries.shape, jnp.bfloat16),
        pltpu.VMEM(keys.shape, jnp.bfloat16),
        pltpu.VMEM(keys.shape, jnp.bfloat16),
        pltpu.VMEM((count, count), jnp.float32),
        pltpu.VMEM((count, 2 * kv_width), jnp.bfloat16),
        pltpu.SemaphoreType.DMA((blocks + 3,)),
    ]
    mixed, state = pl.pallas_call(
        pack_kernel,
        out_shape=(jax.ShapeDtypeStruct(keys.shape, jnp.bfloat16), state_shape),
        in_specs=[SMEM] + [HBM] * 4,
        out_specs=(VMEM,) * 2,
        scratch_shapes=[pltpu.VMEM(segment_ids.shape, jnp.int32), pltpu.SemaphoreType.DMA((3,))] + own_scratch,
        compiler_params=params(10),
        cost_estimate=cost(1),
        name="pack",
    )(place, *in_hbm)
    two_left = lax.ppermute(mixed, "ctx", [(0, 2), (2, 3)])

    state = pl.pallas_call(
        own_kernel,
        out_shape=state_shape,
        in_specs=[SMEM] + [HBM] * 4 + [VMEM],
        out_specs=VMEM,
        scratch_shapes=[pltpu.VMEM(segment_ids.shape, jnp.int32)] + own_scratch,
        input_output_aliases={5: 0},
        compiler_params=params(10),
        cost_estimate=cost(16 * count * count * width),
        name="own",
    )(place, *in_hbm, state)

    keys_2, mixed, state = lax.optimization_barrier((keys_2, mixed, state))
    keys_3 = lax.ppermute(keys_2, "ctx", [(2, 3)])
    keys_1 = lax.ppermute(keys_2, "ctx", [(2, 1)])
    one_left = lax.ppermute(mixed, "ctx", [(0, 1), (1, 2)])
    values_3 = lax.ppermute(two_left, "ctx", [(2, 3)])

    tail_scratch = [pltpu.VMEM((padded, kv_width), jnp.bfloat16), pltpu.VMEM((padded, 2 * kv_width), jnp.bfloat16)]
    state = pl.pallas_call(
        tail_kernel,
        out_shape=state_shape,
        in_specs=[SMEM] + [VMEM] * 4,
        out_specs=VMEM,
        scratch_shapes=tail_scratch,
        input_output_aliases={4: 0},
        compiler_params=params(8),
        cost_estimate=cost(1),
        name="tail",
    )(place, queries, two_left, segment_ids, state)

    out_shape = jax.ShapeDtypeStruct(queries.shape, jnp.bfloat16)
    reached = -(-half // ROWS) * ROWS
    chunks = blocks * (kv_width // HEAD_DIM) + 1
    out_scratch = [pltpu.VMEM(queries.shape, jnp.bfloat16), pltpu.SemaphoreType.DMA((chunks,))]
    wide_scratch = [pltpu.VMEM((count, 2 * kv_width), jnp.bfloat16)]

    def scores(places, key_blocks):
        return pl.pallas_call(
            functools.partial(scores_kernel, places),
            out_shape=(
                jax.ShapeDtypeStruct((count * width // HEAD_DIM, count), jnp.bfloat16),
                jax.ShapeDtypeStruct((count, LANES), jnp.float32),
            ),
            in_specs=[SMEM] + [VMEM] * (1 + len(places)),
            out_specs=(VMEM,) * 2,
            scratch_shapes=[pltpu.VMEM(keys.shape, jnp.bfloat16)],
            compiler_params=params(8),
            cost_estimate=cost(8 * count * count * width),
            name="scores_" + "".join(str(p) for p in places),
        )(place, queries, *key_blocks)

    weights, prompt_peak = scores((2,), (keys_2,))
    out, aux = pl.pallas_call(
        middle_kernel,
        out_shape=(out_shape, jax.ShapeDtypeStruct((reached, 3 * width), jnp.float32)),
        in_specs=[SMEM] + [VMEM] * 4,
        out_specs=(HBM, VMEM),
        scratch_shapes=wide_scratch + out_scratch,
        compiler_params=params(8),
        cost_estimate=cost(1),
        name="middle",
    )(place, weights, two_left, state, prompt_peak)
    weights, prompt_peak = scores((3, 1), (keys_3, keys_1))
    return pl.pallas_call(
        last_kernel,
        out_shape=out_shape,
        in_specs=[SMEM] + [VMEM] * 8 + [HBM],
        out_specs=HBM,
        scratch_shapes=wide_scratch + tail_scratch + out_scratch,
        input_output_aliases={9: 0},
        compiler_params=params(10),
        cost_estimate=cost(1),
        name="last",
    )(place, queries, weights, one_left, values_3, segment_ids, state, prompt_peak, aux, out)


def attend_block(
    running,
    key_block,
    value_block,
    segment_block,
    first_row,
    query_heads,
    query_places,
    query_segment,
):
    number = key_block.shape[0]
    heads_here = key_block.shape[1] // HEAD_DIM
    key_places = first_row + jnp.arange(number, dtype=jnp.int32)
    same = (segment_block[None, :] == query_segment[:, None]) | (segment_block[None, :] == 0)
    visible = (key_places[None, :] <= query_places[:, None]) & same
    key_heads = key_block.reshape(number, heads_here, HEAD_DIM)
    value_heads = value_block.reshape(number, heads_here, HEAD_DIM)

    def compute(state):
        row_peak, row_total, weighted = state
        scores = jnp.einsum(
            "qhgd,khd->hgqk", query_heads, key_heads, preferred_element_type=jnp.float32
        ) * HEAD_DIM ** (-0.5)
        scores = jnp.where(visible[None, None], scores, -1e30)
        new_peak = jnp.maximum(row_peak, jnp.max(scores, axis=-1))
        factor = jnp.exp(row_peak - new_peak)
        weights = jnp.where(visible[None, None], jnp.exp(scores - new_peak[..., None]), 0.0)
        new_total = row_total * factor + jnp.sum(weights, axis=-1)
        added = jnp.einsum(
            "hgqk,khd->hgqd",
            weights.astype(jnp.bfloat16),
            value_heads,
            preferred_element_type=jnp.float32,
        )
        return (new_peak, new_total, weighted * factor[..., None] + added)

    return lax.cond(jnp.any(visible), compute, lambda state: state, running)


def gathered_path(queries, keys, values, segment_ids):
    row_count = queries.shape[0]
    heads_here = keys.shape[1] // HEAD_DIM
    my_index = lax.axis_index("ctx")
    query_places = my_index * row_count + jnp.arange(row_count, dtype=jnp.int32)
    query_heads = queries.reshape(row_count, heads_here, GROUP, HEAD_DIM)
    initial = (
        jnp.full((heads_here, GROUP, row_count), -1e30, jnp.float32),
        jnp.zeros((heads_here, GROUP, row_count), jnp.float32),
        jnp.zeros((heads_here, GROUP, row_count, HEAD_DIM), jnp.float32),
    )
    key_all = lax.all_gather(keys, "ctx", axis=0, tiled=True)
    value_all = lax.all_gather(values, "ctx", axis=0, tiled=True)
    segment_all = lax.all_gather(segment_ids, "ctx", axis=0, tiled=True)
    blocks = max(1, key_all.shape[0] // row_count)
    width_rows = key_all.shape[0] // blocks

    def turn(number, state):
        offset = number * width_rows
        key_part = lax.dynamic_slice_in_dim(key_all, offset, width_rows, 0)
        value_part = lax.dynamic_slice_in_dim(value_all, offset, width_rows, 0)
        segment_part = lax.dynamic_slice_in_dim(segment_all, offset, width_rows, 0)
        return attend_block(
            state, key_part, value_part, segment_part, offset, query_heads, query_places, segment_ids
        )

    row_peak, row_total, weighted = lax.fori_loop(0, blocks, turn, initial)
    mixed = weighted / row_total[..., None]
    mixed = jnp.transpose(mixed, (2, 0, 1, 3)).reshape(row_count, heads_here * GROUP * HEAD_DIM)
    return mixed.astype(jnp.bfloat16)


def per_device(parts, queries, keys, values, segment_ids):
    rows = queries.shape[0]
    tokens = rows * parts
    prompt, chain = tokens // 4, tokens // 8
    if parts == 4 and prompt == rows and 2 * chain == rows and rows % ROWS == 0 and keys.shape[1] >= max(chain, 2 * HEAD_DIM):
        return prompt_block_path(queries, keys, values, segment_ids)
    return gathered_path(queries, keys, values, segment_ids)


def solution(mesh):
    placed = (
        P(("groups", "ctx"), ("tp", "sub")),
        P(("groups", "ctx"), ("tp", "sub")),
        P(("groups", "ctx"), ("tp", "sub")),
        P(("groups", "ctx")),
    )
    return jax.shard_map(
        functools.partial(per_device, mesh.shape["ctx"]),
        mesh=mesh,
        in_specs=placed,
        out_specs=P(("groups", "ctx"), ("tp", "sub")),
        check_vma=False,
    )
```

```python
import functools

import jax
import jax.numpy as jnp
from jax import lax
from jax.experimental import pallas as pl
from jax.experimental.pallas import tpu as pltpu
from jax.sharding import PartitionSpec as P

HEAD_DIM = 128
GROUP = 8
LANES = 128
ROWS = 128
NEG = -1e30
EXP2_SCALE = 1.4426950408889634 * HEAD_DIM ** (-0.5)

VMEM = pl.BlockSpec(memory_space=pltpu.VMEM)
SMEM = pl.BlockSpec(memory_space=pltpu.SMEM)
HBM = pl.BlockSpec(memory_space=pltpu.HBM)


def dot_t(a, b):
    return lax.dot_general(a, b, (((1,), (1,)), ((), ())), preferred_element_type=jnp.float32)


def head_cols(kv_head):
    first = kv_head * GROUP * HEAD_DIM
    return [slice(first + g * HEAD_DIM, first + (g + 1) * HEAD_DIM) for g in range(GROUP)]


def shifted(cols, by):
    return [slice(c.start + by, c.stop + by) for c in cols]


def stack(ref, rows, cols):
    return jnp.concatenate([ref[rows, c] for c in cols], axis=0)


def unstack(ref, rows, cols, value):
    for g, c in enumerate(cols):
        ref[rows, c] = value[g * ROWS : (g + 1) * ROWS].astype(ref.dtype)


def widen(lane_copies, width):
    whole = -(-width // LANES)
    return jnp.concatenate([lane_copies] * whole, axis=1)[:, :width]


def with_ones(wide, source, rows, heads):
    for h in range(heads):
        wide[0:rows, 2 * h * HEAD_DIM : (2 * h + 1) * HEAD_DIM] = source[0:rows, h * HEAD_DIM : (h + 1) * HEAD_DIM]


def fill_ones(wide, heads):
    for h in range(heads):
        wide[:, (2 * h + 1) * HEAD_DIM : (2 * h + 2) * HEAD_DIM] = jnp.ones((wide.shape[0], HEAD_DIM), jnp.bfloat16)


def fetch(source, target, sem):
    copy = pltpu.make_async_copy(source, target, sem)
    copy.start()
    return copy


def pack_kernel(place_ref, q_hbm, k_hbm, v_hbm, seg_hbm, mixed_ref, state, seg_ref, sem, *own_scratch):
    count = k_hbm.shape[0]
    half = count // 2
    place = place_ref[0]
    low, high = pl.ds(0, half), pl.ds(half, half)

    @pl.when(place == 0)
    def _():
        every = fetch(v_hbm, mixed_ref, sem.at[0])
        get_seg = fetch(seg_hbm, seg_ref, sem.at[2])
        attend_own(0, 1, get_seg, q_hbm, k_hbm, v_hbm, state, seg_ref, *own_scratch)
        every.wait()

    @pl.when((place > 0) & (place < 3))
    def _():
        get_seg = fetch(seg_hbm, seg_ref, sem.at[2])
        first = fetch(k_hbm.at[high], mixed_ref.at[low], sem.at[0])
        other = fetch(v_hbm.at[high], mixed_ref.at[high], sem.at[1])
        get_seg.wait()
        seg = seg_ref[...].reshape(1, count).astype(jnp.float32)[:, half:]
        first.wait()
        top = lax.broadcasted_iota(jnp.int32, (16, half), 0) == 0
        old = mixed_ref[0:16, 0:half].astype(jnp.float32)
        mixed_ref[0:16, 0:half] = jnp.where(top, jnp.broadcast_to(seg, (16, half)), old).astype(jnp.bfloat16)
        other.wait()


def attend_own(
    first_head, heads, get_seg, q_hbm, k_hbm, v_hbm, state, seg_ref, q_ref, k_ref, v_ref, bias, wide, in_sem
):
    count, width = q_ref.shape
    blocks = count // ROWS
    span = [slice(b * ROWS, (b + 1) * ROWS) for b in range(blocks)]
    here = slice(first_head * GROUP * HEAD_DIM, (first_head + heads) * GROUP * HEAD_DIM)
    get_k = fetch(k_hbm, k_ref, in_sem.at[blocks])
    get_q = [fetch(q_hbm.at[rows, here], q_ref.at[rows, here], in_sem.at[b]) for b, rows in enumerate(span)]
    get_v = fetch(v_hbm, v_ref, in_sem.at[blocks + 1])
    get_seg.wait()
    seg = seg_ref[...].reshape(1, count).astype(jnp.float32)
    for b in range(blocks):
        of_row = jnp.broadcast_to(seg[:, span[b]], (ROWS, ROWS)).T
        for t in range(b + 1):
            of_key = jnp.broadcast_to(seg[:, span[t]], (ROWS, ROWS))
            seen = (of_key == of_row) | (of_key == 0.0)
            if t == b:
                i = lax.broadcasted_iota(jnp.int32, (ROWS, ROWS), 0)
                j = lax.broadcasted_iota(jnp.int32, (ROWS, ROWS), 1)
                seen = seen & (j <= i)
            bias[span[b], span[t]] = jnp.where(seen, 0.0, NEG)
    fill_ones(wide, k_ref.shape[1] // HEAD_DIM)
    get_k.wait()
    get_v.wait()
    with_ones(wide, v_ref, count, k_ref.shape[1] // HEAD_DIM)
    lane = lax.broadcasted_iota(jnp.int32, (ROWS, LANES), 1)
    for b in range(blocks):
        rows, keys = span[b], (b + 1) * ROWS
        get_q[b].wait()
        if first_head == 0:
            peaks = jnp.zeros((ROWS, LANES), jnp.float32)
            totals = jnp.ones((ROWS, LANES), jnp.float32)
        else:
            peaks = state[rows, width : width + LANES]
            totals = state[rows, width + LANES : width + 2 * LANES]
        for h in range(first_head, first_head + heads):
            cols = head_cols(h)
            scores = dot_t(stack(q_ref, rows, cols), k_ref[0:keys, h * HEAD_DIM : (h + 1) * HEAD_DIM])
            scores = scores.reshape(GROUP, ROWS, keys) + bias[rows, 0:keys][None]
            peak = jnp.max(scores, axis=-1, keepdims=True)
            weights = jnp.exp2((scores - peak) * EXP2_SCALE).astype(jnp.bfloat16).reshape(GROUP * ROWS, keys)
            sums = jnp.dot(
                weights, wide[0:keys, 2 * h * HEAD_DIM : (2 * h + 2) * HEAD_DIM], preferred_element_type=jnp.float32
            )
            unstack(state, rows, cols, sums[:, :HEAD_DIM] / sums[:, HEAD_DIM:])
            for g in range(GROUP):
                mine = lane == h * GROUP + g
                peaks = jnp.where(mine, peak[g], peaks)
                totals = jnp.where(mine, sums[g * ROWS : (g + 1) * ROWS, HEAD_DIM:], totals)
        state[rows, width : width + LANES] = peaks
        state[rows, width + LANES : width + 2 * LANES] = totals


def own_kernel(place_ref, q_hbm, k_hbm, v_hbm, seg_hbm, state_in, state, seg_ref, *scratch):
    heads = k_hbm.shape[1] // HEAD_DIM
    get_seg = fetch(seg_hbm, seg_ref, scratch[-1].at[k_hbm.shape[0] // ROWS + 2])

    @pl.when(place_ref[0] > 0)
    def _():
        attend_own(0, heads, get_seg, q_hbm, k_hbm, v_hbm, state, seg_ref, *scratch)

    @pl.when(place_ref[0] == 0)
    def _():
        attend_own(1, heads - 1, get_seg, q_hbm, k_hbm, v_hbm, state, seg_ref, *scratch)


def scores_kernel(places, place_ref, q_ref, *refs):
    *k_refs, w_ref, peak_ref, k_ref = refs
    count = q_ref.shape[0]
    heads = k_ref.shape[1] // HEAD_DIM
    lane = lax.broadcasted_iota(jnp.int32, (ROWS, LANES), 1)

    place = place_ref[0]

    for here, ref in zip(places, k_refs):

        @pl.when(place == here)
        def _(ref=ref):
            k_ref[...] = ref[...]

    @pl.when(functools.reduce(jnp.logical_or, [place == here for here in places]))
    def _():
        for b in range(count // ROWS):
            rows = slice(b * ROWS, (b + 1) * ROWS)
            peaks = jnp.zeros((ROWS, LANES), jnp.float32)
            for h in range(heads):
                cols = head_cols(h)
                scores = dot_t(stack(q_ref, rows, cols), k_ref[:, h * HEAD_DIM : (h + 1) * HEAD_DIM])
                peak = jnp.max(scores, axis=-1, keepdims=True)
                weights = jnp.exp2((scores - peak) * EXP2_SCALE).astype(jnp.bfloat16)
                first = (h * (count // ROWS) + b) * GROUP * ROWS
                w_ref[first : first + GROUP * ROWS, :] = weights
                for g in range(GROUP):
                    peaks = jnp.where(lane == h * GROUP + g, peak[g * ROWS : (g + 1) * ROWS], peaks)
            peak_ref[rows, :] = peaks


def column(stats, index):
    return jnp.broadcast_to(stats[:, index : index + 1], (stats.shape[0], LANES))


def merge_tail(q_ref, t_ref, seg_ref, peaks_of, tail, wide, finish):
    count, width = q_ref.shape
    heads = width // HEAD_DIM // GROUP
    half = count // 2
    padded = tail.shape[0]
    pad = padded - half
    fill_ones(wide, heads)
    for h in range(heads):
        mine = slice(h * HEAD_DIM, (h + 1) * HEAD_DIM)
        tail[0:pad, mine] = jnp.zeros((pad, HEAD_DIM), jnp.bfloat16)
        tail[pad:padded, mine] = t_ref[0:half, mine]
        wide[0:pad, 2 * h * HEAD_DIM : (2 * h + 1) * HEAD_DIM] = jnp.zeros((pad, HEAD_DIM), jnp.bfloat16)
        wide[pad:padded, 2 * h * HEAD_DIM : (2 * h + 1) * HEAD_DIM] = t_ref[half : 2 * half, mine]
    of_keys = t_ref[0:16, 0:half].astype(jnp.float32)[0:1]
    of_keys = jnp.concatenate([jnp.full((1, pad), -1.0, jnp.float32), of_keys], axis=1)
    of_keys = jnp.where(lax.broadcasted_iota(jnp.int32, (1, padded), 1) <= pad, -1.0, of_keys)
    seg = seg_ref[...].reshape(1, count).astype(jnp.float32)
    for start in range(0, half, ROWS):
        size = min(ROWS, half - start)
        low = (start + pad) // LANES * LANES
        keys = padded - low
        rows = slice(start, start + size)
        of_row = jnp.broadcast_to(seg[:, start : start + ROWS], (ROWS, ROWS)).T[0:size]
        seen = widen(of_row, keys) == jnp.broadcast_to(of_keys[:, low:], (size, keys))
        bias = jnp.where(seen, 0.0, NEG)
        for h in range(heads):
            cols = head_cols(h)
            queries = jnp.concatenate([q_ref[rows, c] for c in cols], axis=0)
            scores = dot_t(queries, tail[low:padded, h * HEAD_DIM : (h + 1) * HEAD_DIM])
            scores = (scores.reshape(GROUP, size, keys) + bias[None]).reshape(GROUP * size, keys)
            own = peaks_of(rows, h)
            peak = jnp.maximum(own, jnp.max(scores, axis=-1, keepdims=True))
            weights = jnp.exp2((scores - widen(peak, keys)) * EXP2_SCALE).astype(jnp.bfloat16)
            sums = jnp.dot(
                weights, wide[low:padded, 2 * h * HEAD_DIM : (2 * h + 2) * HEAD_DIM], preferred_element_type=jnp.float32
            )
            scale = jnp.exp2((own - peak) * EXP2_SCALE)
            finish(rows, h, cols, peak, scale, sums)


def tail_kernel(place_ref, q_ref, t_ref, seg_ref, state_in, state, tail, wide):
    width = q_ref.shape[1]

    def peaks_of(rows, h):
        peaks = state_in[rows, width : width + LANES]
        return jnp.concatenate([column(peaks, h * GROUP + g) for g in range(GROUP)], axis=0)

    def finish(rows, h, cols, peak, scale, sums):
        size = rows.stop - rows.start
        lane = lax.broadcasted_iota(jnp.int32, (size, LANES), 1)
        old_totals = state_in[rows, width + LANES : width + 2 * LANES]
        peaks = state[rows, width : width + LANES]
        totals = state[rows, width + LANES : width + 2 * LANES]
        for g, c in enumerate(cols):
            mine = slice(g * size, (g + 1) * size)
            index = h * GROUP + g
            old = column(old_totals, index) * scale[mine]
            total = old + sums[mine, HEAD_DIM:]
            state[rows, c] = (state[rows, c] * old + sums[mine, :HEAD_DIM]) / total
            peaks = jnp.where(lane == index, peak[mine], peaks)
            totals = jnp.where(lane == index, total, totals)
        state[rows, width : width + LANES] = peaks
        state[rows, width + LANES : width + 2 * LANES] = totals

    @pl.when(place_ref[0] == 3)
    def _():
        merge_tail(q_ref, t_ref, seg_ref, peaks_of, tail, wide, finish)


def prompt_rows(w_ref, state, ppeak_ref, wide, finish):
    count = wide.shape[0]
    heads = wide.shape[1] // 2 // HEAD_DIM
    width = heads * GROUP * HEAD_DIM
    for b in range(count // ROWS):
        rows = slice(b * ROWS, (b + 1) * ROWS)
        own, prompt = state[rows, width : width + LANES], ppeak_ref[rows, :]
        peak = jnp.maximum(own, prompt)
        prompt_scale = jnp.exp2((prompt - peak) * EXP2_SCALE)
        own_total = state[rows, width + LANES : width + 2 * LANES] * jnp.exp2((own - peak) * EXP2_SCALE)
        for h in range(heads):
            first = (h * (count // ROWS) + b) * GROUP * ROWS
            pieces = 4
            size = GROUP // pieces
            for p in range(pieces):
                low = first + p * size * ROWS
                sums = jnp.dot(
                    w_ref[low : low + size * ROWS, :],
                    wide[:, 2 * h * HEAD_DIM : (2 * h + 2) * HEAD_DIM],
                    preferred_element_type=jnp.float32,
                )
                cols = head_cols(h)[p * size : (p + 1) * size]
                for g, c in enumerate(cols):
                    index = h * GROUP + p * size + g
                    mine = slice(g * ROWS, (g + 1) * ROWS)
                    own_part, prompt_part = column(own_total, index), column(prompt_scale, index)
                    total = own_part + sums[mine, HEAD_DIM:] * prompt_part
                    value = (state[rows, c] * own_part + sums[mine, :HEAD_DIM] * prompt_part) / total
                    finish(rows, c, value, index, peak, total)
                finish(rows, slice(cols[0].start, cols[-1].stop), None, None, None, None)


def middle_kernel(place_ref, w_ref, v_ref, state, ppeak_ref, out_ref, aux, wide, staged, sem):
    width = staged.shape[1]
    heads = width // HEAD_DIM // GROUP

    @pl.when(place_ref[0] == 2)
    def _():
        def finish(rows, cols, value, index, peak, total):
            goes_on = rows.stop <= aux.shape[0]
            if value is None:
                if not goes_on:
                    put_out(staged, out_ref, sem, rows, cols)
            elif goes_on:
                aux[rows, cols] = value
                aux[rows, shifted([cols], width)[0]] = column(peak, index)
                aux[rows, shifted([cols], 2 * width)[0]] = total
            else:
                staged[rows, cols] = value.astype(jnp.bfloat16)

        fill_ones(wide, heads)
        with_ones(wide, v_ref, staged.shape[0], heads)
        prompt_rows(w_ref, state, ppeak_ref, wide, finish)
        if aux.shape[0] < staged.shape[0]:
            wait_out(staged, out_ref, sem, aux.shape[0], staged.shape[0] - aux.shape[0])


def put_out(staged, out_ref, sem, rows, cols):
    box = (pl.ds(rows.start, rows.stop - rows.start), pl.ds(cols.start, cols.stop - cols.start))
    fetch(staged.at[box], out_ref.at[box], sem)


def wait_out(staged, out_ref, sem, first, number):
    rows = pl.ds(first, number)
    pltpu.make_async_copy(staged.at[rows], out_ref.at[rows], sem).wait()


def last_kernel(
    place_ref, q_ref, w_ref, one_ref, v3_ref, seg_ref, state, ppeak_ref, aux, out_in, out_ref, wide, tail, tail_wide, staged, sem
):
    count, width = q_ref.shape
    heads = width // HEAD_DIM // GROUP
    half = count // 2
    place = place_ref[0]

    def run(body, number):
        body(functools.partial(put_out, staged, out_ref, sem))
        wait_out(staged, out_ref, sem, 0, number)

    @pl.when(place == 0)
    def _():
        def body(put):
            for b in range(count // ROWS):
                rows = slice(b * ROWS, (b + 1) * ROWS)
                staged[rows, :] = state[rows, 0:width].astype(jnp.bfloat16)
                put(rows, slice(0, width))

        run(body, count)

    for here, ref in ((1, one_ref), (3, v3_ref)):
        pl.when(place == here)(functools.partial(with_ones, wide, ref, count, heads))

    @pl.when((place == 1) | (place == 3))
    def _():
        fill_ones(wide, heads)

        def body(put):
            def finish(rows, cols, value, index, peak, total):
                if value is None:
                    put(rows, cols)
                else:
                    staged[rows, cols] = value.astype(jnp.bfloat16)

            prompt_rows(w_ref, state, ppeak_ref, wide, finish)

        run(body, count)

    @pl.when(place == 2)
    def _():
        def body(put):
            def peaks_of(rows, h):
                return stack(aux, rows, shifted(head_cols(h), width))

            def finish(rows, h, cols, peak, scale, sums):
                size = rows.stop - rows.start
                for g, c in enumerate(cols):
                    mine = slice(g * size, (g + 1) * size)
                    total = aux[rows, shifted([c], 2 * width)[0]] * scale[mine]
                    value = (aux[rows, c] * total + sums[mine, :HEAD_DIM]) / (total + sums[mine, HEAD_DIM:])
                    staged[rows, c] = value.astype(jnp.bfloat16)
                put(rows, slice(cols[0].start, cols[-1].stop))

            if aux.shape[0] > half:
                rest = slice(half, aux.shape[0])
                staged[rest, :] = aux[rest, 0:width].astype(jnp.bfloat16)
                put(rest, slice(0, width))
            merge_tail(q_ref, one_ref, seg_ref, peaks_of, tail, tail_wide, finish)

        run(body, aux.shape[0])


def params(mebibytes):
    return pltpu.CompilerParams(vmem_limit_bytes=mebibytes << 20)


def cost(flops):
    return pl.CostEstimate(flops=flops, bytes_accessed=1, transcendentals=0)


def prompt_block_path(queries, keys, values, segment_ids):
    count, kv_width = keys.shape
    width = queries.shape[1]
    half = count // 2
    padded = -(-half // LANES) * LANES
    blocks = count // ROWS
    place = lax.axis_index("ctx").astype(jnp.int32).reshape(1)
    in_hbm = [pltpu.with_memory_space_constraint(x, pltpu.HBM) for x in (queries, keys, values, segment_ids)]

    keys_2 = lax.ppermute(keys, "ctx", [(0, 2)])
    state_shape = jax.ShapeDtypeStruct((count, width + 2 * LANES), jnp.float32)
    own_scratch = [
        pltpu.VMEM(queries.shape, jnp.bfloat16),
        pltpu.VMEM(keys.shape, jnp.bfloat16),
        pltpu.VMEM(keys.shape, jnp.bfloat16),
        pltpu.VMEM((count, count), jnp.float32),
        pltpu.VMEM((count, 2 * kv_width), jnp.bfloat16),
        pltpu.SemaphoreType.DMA((blocks + 3,)),
    ]
    mixed, state = pl.pallas_call(
        pack_kernel,
        out_shape=(jax.ShapeDtypeStruct(keys.shape, jnp.bfloat16), state_shape),
        in_specs=[SMEM] + [HBM] * 4,
        out_specs=(VMEM,) * 2,
        scratch_shapes=[pltpu.VMEM(segment_ids.shape, jnp.int32), pltpu.SemaphoreType.DMA((3,))] + own_scratch,
        compiler_params=params(10),
        cost_estimate=cost(1),
        name="pack",
    )(place, *in_hbm)
    two_left = lax.ppermute(mixed, "ctx", [(0, 2), (2, 3)])

    state = pl.pallas_call(
        own_kernel,
        out_shape=state_shape,
        in_specs=[SMEM] + [HBM] * 4 + [VMEM],
        out_specs=VMEM,
        scratch_shapes=[pltpu.VMEM(segment_ids.shape, jnp.int32)] + own_scratch,
        input_output_aliases={5: 0},
        compiler_params=params(10),
        cost_estimate=cost(16 * count * count * width),
        name="own",
    )(place, *in_hbm, state)

    keys_2, mixed, state = lax.optimization_barrier((keys_2, mixed, state))
    keys_3 = lax.ppermute(keys_2, "ctx", [(2, 3)])
    keys_1 = lax.ppermute(keys_2, "ctx", [(2, 1)])
    one_left = lax.ppermute(mixed, "ctx", [(0, 1), (1, 2)])
    values_3 = lax.ppermute(two_left, "ctx", [(2, 3)])

    tail_scratch = [pltpu.VMEM((padded, kv_width), jnp.bfloat16), pltpu.VMEM((padded, 2 * kv_width), jnp.bfloat16)]
    state = pl.pallas_call(
        tail_kernel,
        out_shape=state_shape,
        in_specs=[SMEM] + [VMEM] * 4,
        out_specs=VMEM,
        scratch_shapes=tail_scratch,
        input_output_aliases={4: 0},
        compiler_params=params(8),
        cost_estimate=cost(1),
        name="tail",
    )(place, queries, two_left, segment_ids, state)

    out_shape = jax.ShapeDtypeStruct(queries.shape, jnp.bfloat16)
    reached = -(-half // ROWS) * ROWS
    out_scratch = [pltpu.VMEM(queries.shape, jnp.bfloat16), pltpu.SemaphoreType.DMA]
    wide_scratch = [pltpu.VMEM((count, 2 * kv_width), jnp.bfloat16)]

    def scores(places, key_blocks):
        return pl.pallas_call(
            functools.partial(scores_kernel, places),
            out_shape=(
                jax.ShapeDtypeStruct((count * width // HEAD_DIM, count), jnp.bfloat16),
                jax.ShapeDtypeStruct((count, LANES), jnp.float32),
            ),
            in_specs=[SMEM] + [VMEM] * (1 + len(places)),
            out_specs=(VMEM,) * 2,
            scratch_shapes=[pltpu.VMEM(keys.shape, jnp.bfloat16)],
            compiler_params=params(8),
            cost_estimate=cost(8 * count * count * width),
            name="scores_" + "".join(str(p) for p in places),
        )(place, queries, *key_blocks)

    weights, prompt_peak = scores((2,), (keys_2,))
    out, aux = pl.pallas_call(
        middle_kernel,
        out_shape=(out_shape, jax.ShapeDtypeStruct((reached, 3 * width), jnp.float32)),
        in_specs=[SMEM] + [VMEM] * 4,
        out_specs=(HBM, VMEM),
        scratch_shapes=wide_scratch + out_scratch,
        compiler_params=params(8),
        cost_estimate=cost(1),
        name="middle",
    )(place, weights, two_left, state, prompt_peak)
    weights, prompt_peak = scores((3, 1), (keys_3, keys_1))
    return pl.pallas_call(
        last_kernel,
        out_shape=out_shape,
        in_specs=[SMEM] + [VMEM] * 8 + [HBM],
        out_specs=HBM,
        scratch_shapes=wide_scratch + tail_scratch + out_scratch,
        input_output_aliases={9: 0},
        compiler_params=params(10),
        cost_estimate=cost(1),
        name="last",
    )(place, queries, weights, one_left, values_3, segment_ids, state, prompt_peak, aux, out)


def attend_block(
    running,
    key_block,
    value_block,
    segment_block,
    first_row,
    query_heads,
    query_places,
    query_segment,
):
    number = key_block.shape[0]
    heads_here = key_block.shape[1] // HEAD_DIM
    key_places = first_row + jnp.arange(number, dtype=jnp.int32)
    same = (segment_block[None, :] == query_segment[:, None]) | (segment_block[None, :] == 0)
    visible = (key_places[None, :] <= query_places[:, None]) & same
    key_heads = key_block.reshape(number, heads_here, HEAD_DIM)
    value_heads = value_block.reshape(number, heads_here, HEAD_DIM)

    def compute(state):
        row_peak, row_total, weighted = state
        scores = jnp.einsum(
            "qhgd,khd->hgqk", query_heads, key_heads, preferred_element_type=jnp.float32
        ) * HEAD_DIM ** (-0.5)
        scores = jnp.where(visible[None, None], scores, -1e30)
        new_peak = jnp.maximum(row_peak, jnp.max(scores, axis=-1))
        factor = jnp.exp(row_peak - new_peak)
        weights = jnp.where(visible[None, None], jnp.exp(scores - new_peak[..., None]), 0.0)
        new_total = row_total * factor + jnp.sum(weights, axis=-1)
        added = jnp.einsum(
            "hgqk,khd->hgqd",
            weights.astype(jnp.bfloat16),
            value_heads,
            preferred_element_type=jnp.float32,
        )
        return (new_peak, new_total, weighted * factor[..., None] + added)

    return lax.cond(jnp.any(visible), compute, lambda state: state, running)


def gathered_path(queries, keys, values, segment_ids):
    row_count = queries.shape[0]
    heads_here = keys.shape[1] // HEAD_DIM
    my_index = lax.axis_index("ctx")
    query_places = my_index * row_count + jnp.arange(row_count, dtype=jnp.int32)
    query_heads = queries.reshape(row_count, heads_here, GROUP, HEAD_DIM)
    initial = (
        jnp.full((heads_here, GROUP, row_count), -1e30, jnp.float32),
        jnp.zeros((heads_here, GROUP, row_count), jnp.float32),
        jnp.zeros((heads_here, GROUP, row_count, HEAD_DIM), jnp.float32),
    )
    key_all = lax.all_gather(keys, "ctx", axis=0, tiled=True)
    value_all = lax.all_gather(values, "ctx", axis=0, tiled=True)
    segment_all = lax.all_gather(segment_ids, "ctx", axis=0, tiled=True)
    blocks = max(1, key_all.shape[0] // row_count)
    width_rows = key_all.shape[0] // blocks

    def turn(number, state):
        offset = number * width_rows
        key_part = lax.dynamic_slice_in_dim(key_all, offset, width_rows, 0)
        value_part = lax.dynamic_slice_in_dim(value_all, offset, width_rows, 0)
        segment_part = lax.dynamic_slice_in_dim(segment_all, offset, width_rows, 0)
        return attend_block(
            state, key_part, value_part, segment_part, offset, query_heads, query_places, segment_ids
        )

    row_peak, row_total, weighted = lax.fori_loop(0, blocks, turn, initial)
    mixed = weighted / row_total[..., None]
    mixed = jnp.transpose(mixed, (2, 0, 1, 3)).reshape(row_count, heads_here * GROUP * HEAD_DIM)
    return mixed.astype(jnp.bfloat16)


def per_device(parts, queries, keys, values, segment_ids):
    rows = queries.shape[0]
    tokens = rows * parts
    prompt, chain = tokens // 4, tokens // 8
    if parts == 4 and prompt == rows and 2 * chain == rows and rows % ROWS == 0 and keys.shape[1] >= max(chain, 2 * HEAD_DIM):
        return prompt_block_path(queries, keys, values, segment_ids)
    return gathered_path(queries, keys, values, segment_ids)


def solution(mesh):
    placed = (
        P(("groups", "ctx"), ("tp", "sub")),
        P(("groups", "ctx"), ("tp", "sub")),
        P(("groups", "ctx"), ("tp", "sub")),
        P(("groups", "ctx")),
    )
    return jax.shard_map(
        functools.partial(per_device, mesh.shape["ctx"]),
        mesh=mesh,
        in_specs=placed,
        out_specs=P(("groups", "ctx"), ("tp", "sub")),
        check_vma=False,
    )
```

```python
import functools

import jax
import jax.numpy as jnp
from jax import lax
from jax.experimental import pallas as pl
from jax.experimental.pallas import tpu as pltpu
from jax.sharding import PartitionSpec as P

HEAD_DIM = 128
GROUP = 8
LANES = 128
ROWS = 128
NEG = -1e30
EXP2_SCALE = 1.4426950408889634 * HEAD_DIM ** (-0.5)

VMEM = pl.BlockSpec(memory_space=pltpu.VMEM)
SMEM = pl.BlockSpec(memory_space=pltpu.SMEM)
HBM = pl.BlockSpec(memory_space=pltpu.HBM)


def dot_t(a, b):
    return lax.dot_general(a, b, (((1,), (1,)), ((), ())), preferred_element_type=jnp.float32)


def head_cols(kv_head):
    first = kv_head * GROUP * HEAD_DIM
    return [slice(first + g * HEAD_DIM, first + (g + 1) * HEAD_DIM) for g in range(GROUP)]


def shifted(cols, by):
    return [slice(c.start + by, c.stop + by) for c in cols]


def stack(ref, rows, cols):
    return jnp.concatenate([ref[rows, c] for c in cols], axis=0)


def unstack(ref, rows, cols, value):
    for g, c in enumerate(cols):
        ref[rows, c] = value[g * ROWS : (g + 1) * ROWS].astype(ref.dtype)


def widen(lane_copies, width):
    whole = -(-width // LANES)
    return jnp.concatenate([lane_copies] * whole, axis=1)[:, :width]


def with_ones(wide, source, rows, heads):
    for h in range(heads):
        wide[0:rows, 2 * h * HEAD_DIM : (2 * h + 1) * HEAD_DIM] = source[0:rows, h * HEAD_DIM : (h + 1) * HEAD_DIM]


def fill_ones(wide, heads):
    for h in range(heads):
        wide[:, (2 * h + 1) * HEAD_DIM : (2 * h + 2) * HEAD_DIM] = jnp.ones((wide.shape[0], HEAD_DIM), jnp.bfloat16)


def fetch(source, target, sem):
    copy = pltpu.make_async_copy(source, target, sem)
    copy.start()
    return copy


def pack_kernel(place_ref, q_hbm, k_hbm, v_hbm, seg_hbm, mixed_ref, state, seg_ref, sem, *own_scratch):
    count = k_hbm.shape[0]
    half = count // 2
    place = place_ref[0]
    low, high = pl.ds(0, half), pl.ds(half, half)

    @pl.when(place == 0)
    def _():
        every = fetch(v_hbm, mixed_ref, sem.at[0])
        get_seg = fetch(seg_hbm, seg_ref, sem.at[2])
        attend_own(0, 1, get_seg, q_hbm, k_hbm, v_hbm, state, seg_ref, *own_scratch)
        every.wait()

    @pl.when((place > 0) & (place < 3))
    def _():
        get_seg = fetch(seg_hbm, seg_ref, sem.at[2])
        first = fetch(k_hbm.at[high], mixed_ref.at[low], sem.at[0])
        other = fetch(v_hbm.at[high], mixed_ref.at[high], sem.at[1])
        get_seg.wait()
        seg = seg_ref[...].reshape(1, count).astype(jnp.float32)[:, half:]
        first.wait()
        top = lax.broadcasted_iota(jnp.int32, (16, half), 0) == 0
        old = mixed_ref[0:16, 0:half].astype(jnp.float32)
        mixed_ref[0:16, 0:half] = jnp.where(top, jnp.broadcast_to(seg, (16, half)), old).astype(jnp.bfloat16)
        other.wait()


def attend_own(
    first_head, heads, get_seg, q_hbm, k_hbm, v_hbm, state, seg_ref, q_ref, k_ref, v_ref, bias, wide, in_sem
):
    count, width = q_ref.shape
    blocks = count // ROWS
    span = [slice(b * ROWS, (b + 1) * ROWS) for b in range(blocks)]
    here = slice(first_head * GROUP * HEAD_DIM, (first_head + heads) * GROUP * HEAD_DIM)
    get_k = fetch(k_hbm, k_ref, in_sem.at[blocks])
    get_q = [fetch(q_hbm.at[rows, here], q_ref.at[rows, here], in_sem.at[b]) for b, rows in enumerate(span)]
    get_v = fetch(v_hbm, v_ref, in_sem.at[blocks + 1])
    get_seg.wait()
    seg = seg_ref[...].reshape(1, count).astype(jnp.float32)
    for b in range(blocks):
        of_row = jnp.broadcast_to(seg[:, span[b]], (ROWS, ROWS)).T
        for t in range(b + 1):
            of_key = jnp.broadcast_to(seg[:, span[t]], (ROWS, ROWS))
            seen = (of_key == of_row) | (of_key == 0.0)
            if t == b:
                i = lax.broadcasted_iota(jnp.int32, (ROWS, ROWS), 0)
                j = lax.broadcasted_iota(jnp.int32, (ROWS, ROWS), 1)
                seen = seen & (j <= i)
            bias[span[b], span[t]] = jnp.where(seen, 0.0, NEG)
    fill_ones(wide, k_ref.shape[1] // HEAD_DIM)
    get_k.wait()
    get_v.wait()
    with_ones(wide, v_ref, count, k_ref.shape[1] // HEAD_DIM)
    lane = lax.broadcasted_iota(jnp.int32, (ROWS, LANES), 1)
    for b in range(blocks):
        rows, keys = span[b], (b + 1) * ROWS
        get_q[b].wait()
        if first_head == 0:
            peaks = jnp.zeros((ROWS, LANES), jnp.float32)
            totals = jnp.ones((ROWS, LANES), jnp.float32)
        else:
            peaks = state[rows, width : width + LANES]
            totals = state[rows, width + LANES : width + 2 * LANES]
        for h in range(first_head, first_head + heads):
            cols = head_cols(h)
            scores = dot_t(stack(q_ref, rows, cols), k_ref[0:keys, h * HEAD_DIM : (h + 1) * HEAD_DIM])
            scores = scores.reshape(GROUP, ROWS, keys) + bias[rows, 0:keys][None]
            peak = jnp.max(scores, axis=-1, keepdims=True)
            weights = jnp.exp2((scores - peak) * EXP2_SCALE).astype(jnp.bfloat16).reshape(GROUP * ROWS, keys)
            sums = jnp.dot(
                weights, wide[0:keys, 2 * h * HEAD_DIM : (2 * h + 2) * HEAD_DIM], preferred_element_type=jnp.float32
            )
            unstack(state, rows, cols, sums[:, :HEAD_DIM] / sums[:, HEAD_DIM:])
            for g in range(GROUP):
                mine = lane == h * GROUP + g
                peaks = jnp.where(mine, peak[g], peaks)
                totals = jnp.where(mine, sums[g * ROWS : (g + 1) * ROWS, HEAD_DIM:], totals)
        state[rows, width : width + LANES] = peaks
        state[rows, width + LANES : width + 2 * LANES] = totals


def own_kernel(place_ref, q_hbm, k_hbm, v_hbm, seg_hbm, state_in, state, seg_ref, *scratch):
    heads = k_hbm.shape[1] // HEAD_DIM
    get_seg = fetch(seg_hbm, seg_ref, scratch[-1].at[k_hbm.shape[0] // ROWS + 2])

    @pl.when(place_ref[0] > 0)
    def _():
        attend_own(0, heads, get_seg, q_hbm, k_hbm, v_hbm, state, seg_ref, *scratch)

    @pl.when(place_ref[0] == 0)
    def _():
        attend_own(1, heads - 1, get_seg, q_hbm, k_hbm, v_hbm, state, seg_ref, *scratch)


def scores_kernel(places, place_ref, q_ref, *refs):
    *k_refs, w_ref, peak_ref, k_ref = refs
    count = q_ref.shape[0]
    heads = k_ref.shape[1] // HEAD_DIM
    lane = lax.broadcasted_iota(jnp.int32, (ROWS, LANES), 1)

    place = place_ref[0]

    for here, ref in zip(places, k_refs):

        @pl.when(place == here)
        def _(ref=ref):
            k_ref[...] = ref[...]

    @pl.when(functools.reduce(jnp.logical_or, [place == here for here in places]))
    def _():
        for b in range(count // ROWS):
            rows = slice(b * ROWS, (b + 1) * ROWS)
            peaks = jnp.zeros((ROWS, LANES), jnp.float32)
            for h in range(heads):
                for low in range(0, GROUP, 2):
                    cols = head_cols(h)[low : low + 2]
                    scores = dot_t(stack(q_ref, rows, cols), k_ref[:, h * HEAD_DIM : (h + 1) * HEAD_DIM])
                    peak = jnp.max(scores, axis=-1, keepdims=True)
                    weights = jnp.exp2((scores - peak) * EXP2_SCALE).astype(jnp.bfloat16)
                    first = ((h * (count // ROWS) + b) * GROUP + low) * ROWS
                    w_ref[first : first + 2 * ROWS, :] = weights
                    for g in range(2):
                        here = lane == h * GROUP + low + g
                        peaks = jnp.where(here, peak[g * ROWS : (g + 1) * ROWS], peaks)
            peak_ref[rows, :] = peaks


def column(stats, index):
    return jnp.broadcast_to(stats[:, index : index + 1], (stats.shape[0], LANES))


def merge_tail(q_ref, t_ref, seg_ref, peaks_of, tail, wide, finish):
    count, width = q_ref.shape
    heads = width // HEAD_DIM // GROUP
    half = count // 2
    padded = tail.shape[0]
    pad = padded - half
    fill_ones(wide, heads)
    for h in range(heads):
        mine = slice(h * HEAD_DIM, (h + 1) * HEAD_DIM)
        tail[0:pad, mine] = jnp.zeros((pad, HEAD_DIM), jnp.bfloat16)
        tail[pad:padded, mine] = t_ref[0:half, mine]
        wide[0:pad, 2 * h * HEAD_DIM : (2 * h + 1) * HEAD_DIM] = jnp.zeros((pad, HEAD_DIM), jnp.bfloat16)
        wide[pad:padded, 2 * h * HEAD_DIM : (2 * h + 1) * HEAD_DIM] = t_ref[half : 2 * half, mine]
    of_keys = t_ref[0:16, 0:half].astype(jnp.float32)[0:1]
    of_keys = jnp.concatenate([jnp.full((1, pad), -1.0, jnp.float32), of_keys], axis=1)
    of_keys = jnp.where(lax.broadcasted_iota(jnp.int32, (1, padded), 1) <= pad, -1.0, of_keys)
    seg = seg_ref[...].reshape(1, count).astype(jnp.float32)
    for start in range(0, half, ROWS):
        size = min(ROWS, half - start)
        low = (start + pad) // LANES * LANES
        keys = padded - low
        rows = slice(start, start + size)
        of_row = jnp.broadcast_to(seg[:, start : start + ROWS], (ROWS, ROWS)).T[0:size]
        seen = widen(of_row, keys) == jnp.broadcast_to(of_keys[:, low:], (size, keys))
        bias = jnp.where(seen, 0.0, NEG)
        for h in range(heads):
            cols = head_cols(h)
            queries = jnp.concatenate([q_ref[rows, c] for c in cols], axis=0)
            scores = dot_t(queries, tail[low:padded, h * HEAD_DIM : (h + 1) * HEAD_DIM])
            scores = (scores.reshape(GROUP, size, keys) + bias[None]).reshape(GROUP * size, keys)
            own = peaks_of(rows, h)
            peak = jnp.maximum(own, jnp.max(scores, axis=-1, keepdims=True))
            weights = jnp.exp2((scores - widen(peak, keys)) * EXP2_SCALE).astype(jnp.bfloat16)
            sums = jnp.dot(
                weights, wide[low:padded, 2 * h * HEAD_DIM : (2 * h + 2) * HEAD_DIM], preferred_element_type=jnp.float32
            )
            scale = jnp.exp2((own - peak) * EXP2_SCALE)
            finish(rows, h, cols, peak, scale, sums)


def tail_kernel(place_ref, q_ref, t_ref, seg_ref, state_in, state, tail, wide):
    width = q_ref.shape[1]

    def peaks_of(rows, h):
        peaks = state_in[rows, width : width + LANES]
        return jnp.concatenate([column(peaks, h * GROUP + g) for g in range(GROUP)], axis=0)

    def finish(rows, h, cols, peak, scale, sums):
        size = rows.stop - rows.start
        lane = lax.broadcasted_iota(jnp.int32, (size, LANES), 1)
        old_totals = state_in[rows, width + LANES : width + 2 * LANES]
        peaks = state[rows, width : width + LANES]
        totals = state[rows, width + LANES : width + 2 * LANES]
        for g, c in enumerate(cols):
            mine = slice(g * size, (g + 1) * size)
            index = h * GROUP + g
            old = column(old_totals, index) * scale[mine]
            total = old + sums[mine, HEAD_DIM:]
            state[rows, c] = (state[rows, c] * old + sums[mine, :HEAD_DIM]) / total
            peaks = jnp.where(lane == index, peak[mine], peaks)
            totals = jnp.where(lane == index, total, totals)
        state[rows, width : width + LANES] = peaks
        state[rows, width + LANES : width + 2 * LANES] = totals

    @pl.when(place_ref[0] == 3)
    def _():
        merge_tail(q_ref, t_ref, seg_ref, peaks_of, tail, wide, finish)


def prompt_rows(w_ref, state, ppeak_ref, wide, finish):
    count = wide.shape[0]
    heads = wide.shape[1] // 2 // HEAD_DIM
    width = heads * GROUP * HEAD_DIM
    for b in range(count // ROWS):
        rows = slice(b * ROWS, (b + 1) * ROWS)
        own, prompt = state[rows, width : width + LANES], ppeak_ref[rows, :]
        peak = jnp.maximum(own, prompt)
        prompt_scale = jnp.exp2((prompt - peak) * EXP2_SCALE)
        own_total = state[rows, width + LANES : width + 2 * LANES] * jnp.exp2((own - peak) * EXP2_SCALE)
        for h in range(heads):
            first = (h * (count // ROWS) + b) * GROUP * ROWS
            pieces = 4
            size = GROUP // pieces
            for p in range(pieces):
                low = first + p * size * ROWS
                sums = jnp.dot(
                    w_ref[low : low + size * ROWS, :],
                    wide[:, 2 * h * HEAD_DIM : (2 * h + 2) * HEAD_DIM],
                    preferred_element_type=jnp.float32,
                )
                cols = head_cols(h)[p * size : (p + 1) * size]
                for g, c in enumerate(cols):
                    index = h * GROUP + p * size + g
                    mine = slice(g * ROWS, (g + 1) * ROWS)
                    own_part, prompt_part = column(own_total, index), column(prompt_scale, index)
                    total = own_part + sums[mine, HEAD_DIM:] * prompt_part
                    value = (state[rows, c] * own_part + sums[mine, :HEAD_DIM] * prompt_part) / total
                    finish(rows, c, value, index, peak, total)
                finish(rows, slice(cols[0].start, cols[-1].stop), None, None, None, None)


def middle_kernel(place_ref, w_ref, v_ref, state, ppeak_ref, out_ref, aux, wide, staged, sem):
    width = staged.shape[1]
    heads = width // HEAD_DIM // GROUP

    @pl.when(place_ref[0] == 2)
    def _():
        def finish(rows, cols, value, index, peak, total):
            goes_on = rows.stop <= aux.shape[0]
            if value is None:
                if not goes_on:
                    put_out(staged, out_ref, sem, rows, cols)
            elif goes_on:
                aux[rows, cols] = value
                aux[rows, shifted([cols], width)[0]] = column(peak, index)
                aux[rows, shifted([cols], 2 * width)[0]] = total
            else:
                staged[rows, cols] = value.astype(jnp.bfloat16)

        fill_ones(wide, heads)
        with_ones(wide, v_ref, staged.shape[0], heads)
        prompt_rows(w_ref, state, ppeak_ref, wide, finish)
        if aux.shape[0] < staged.shape[0]:
            wait_out(staged, out_ref, sem, aux.shape[0], staged.shape[0] - aux.shape[0])


def put_out(staged, out_ref, sem, rows, cols):
    box = (pl.ds(rows.start, rows.stop - rows.start), pl.ds(cols.start, cols.stop - cols.start))
    fetch(staged.at[box], out_ref.at[box], sem)


def wait_out(staged, out_ref, sem, first, number):
    rows = pl.ds(first, number)
    pltpu.make_async_copy(staged.at[rows], out_ref.at[rows], sem).wait()


def last_kernel(
    place_ref, q_ref, w_ref, one_ref, v3_ref, seg_ref, state, ppeak_ref, aux, out_in, out_ref, wide, tail, tail_wide, staged, sem
):
    count, width = q_ref.shape
    heads = width // HEAD_DIM // GROUP
    half = count // 2
    place = place_ref[0]

    def run(body, number):
        body(functools.partial(put_out, staged, out_ref, sem))
        wait_out(staged, out_ref, sem, 0, number)

    @pl.when(place == 0)
    def _():
        def body(put):
            for b in range(count // ROWS):
                rows = slice(b * ROWS, (b + 1) * ROWS)
                staged[rows, :] = state[rows, 0:width].astype(jnp.bfloat16)
                put(rows, slice(0, width))

        run(body, count)

    for here, ref in ((1, one_ref), (3, v3_ref)):
        pl.when(place == here)(functools.partial(with_ones, wide, ref, count, heads))

    @pl.when((place == 1) | (place == 3))
    def _():
        fill_ones(wide, heads)

        def body(put):
            def finish(rows, cols, value, index, peak, total):
                if value is None:
                    put(rows, cols)
                else:
                    staged[rows, cols] = value.astype(jnp.bfloat16)

            prompt_rows(w_ref, state, ppeak_ref, wide, finish)

        run(body, count)

    @pl.when(place == 2)
    def _():
        def body(put):
            def peaks_of(rows, h):
                return stack(aux, rows, shifted(head_cols(h), width))

            def finish(rows, h, cols, peak, scale, sums):
                size = rows.stop - rows.start
                for g, c in enumerate(cols):
                    mine = slice(g * size, (g + 1) * size)
                    total = aux[rows, shifted([c], 2 * width)[0]] * scale[mine]
                    value = (aux[rows, c] * total + sums[mine, :HEAD_DIM]) / (total + sums[mine, HEAD_DIM:])
                    staged[rows, c] = value.astype(jnp.bfloat16)
                put(rows, slice(cols[0].start, cols[-1].stop))

            if aux.shape[0] > half:
                rest = slice(half, aux.shape[0])
                staged[rest, :] = aux[rest, 0:width].astype(jnp.bfloat16)
                put(rest, slice(0, width))
            merge_tail(q_ref, one_ref, seg_ref, peaks_of, tail, tail_wide, finish)

        run(body, aux.shape[0])


def params(mebibytes):
    return pltpu.CompilerParams(vmem_limit_bytes=mebibytes << 20)


def cost(flops):
    return pl.CostEstimate(flops=flops, bytes_accessed=1, transcendentals=0)


def prompt_block_path(queries, keys, values, segment_ids):
    count, kv_width = keys.shape
    width = queries.shape[1]
    half = count // 2
    padded = -(-half // LANES) * LANES
    blocks = count // ROWS
    place = lax.axis_index("ctx").astype(jnp.int32).reshape(1)
    in_hbm = [pltpu.with_memory_space_constraint(x, pltpu.HBM) for x in (queries, keys, values, segment_ids)]

    keys_2 = lax.ppermute(keys, "ctx", [(0, 2)])
    state_shape = jax.ShapeDtypeStruct((count, width + 2 * LANES), jnp.float32)
    own_scratch = [
        pltpu.VMEM(queries.shape, jnp.bfloat16),
        pltpu.VMEM(keys.shape, jnp.bfloat16),
        pltpu.VMEM(keys.shape, jnp.bfloat16),
        pltpu.VMEM((count, count), jnp.float32),
        pltpu.VMEM((count, 2 * kv_width), jnp.bfloat16),
        pltpu.SemaphoreType.DMA((blocks + 3,)),
    ]
    mixed, state = pl.pallas_call(
        pack_kernel,
        out_shape=(jax.ShapeDtypeStruct(keys.shape, jnp.bfloat16), state_shape),
        in_specs=[SMEM] + [HBM] * 4,
        out_specs=(VMEM,) * 2,
        scratch_shapes=[pltpu.VMEM(segment_ids.shape, jnp.int32), pltpu.SemaphoreType.DMA((3,))] + own_scratch,
        compiler_params=params(10),
        cost_estimate=cost(1),
        name="pack",
    )(place, *in_hbm)
    two_left = lax.ppermute(mixed, "ctx", [(0, 2), (2, 3)])

    state = pl.pallas_call(
        own_kernel,
        out_shape=state_shape,
        in_specs=[SMEM] + [HBM] * 4 + [VMEM],
        out_specs=VMEM,
        scratch_shapes=[pltpu.VMEM(segment_ids.shape, jnp.int32)] + own_scratch,
        input_output_aliases={5: 0},
        compiler_params=params(10),
        cost_estimate=cost(16 * count * count * width),
        name="own",
    )(place, *in_hbm, state)

    keys_2, mixed, state = lax.optimization_barrier((keys_2, mixed, state))
    keys_3 = lax.ppermute(keys_2, "ctx", [(2, 3)])
    keys_1 = lax.ppermute(keys_2, "ctx", [(2, 1)])
    one_left = lax.ppermute(mixed, "ctx", [(0, 1), (1, 2)])
    values_3 = lax.ppermute(two_left, "ctx", [(2, 3)])

    tail_scratch = [pltpu.VMEM((padded, kv_width), jnp.bfloat16), pltpu.VMEM((padded, 2 * kv_width), jnp.bfloat16)]
    state = pl.pallas_call(
        tail_kernel,
        out_shape=state_shape,
        in_specs=[SMEM] + [VMEM] * 4,
        out_specs=VMEM,
        scratch_shapes=tail_scratch,
        input_output_aliases={4: 0},
        compiler_params=params(8),
        cost_estimate=cost(1),
        name="tail",
    )(place, queries, two_left, segment_ids, state)

    out_shape = jax.ShapeDtypeStruct(queries.shape, jnp.bfloat16)
    reached = -(-half // ROWS) * ROWS
    out_scratch = [pltpu.VMEM(queries.shape, jnp.bfloat16), pltpu.SemaphoreType.DMA]
    wide_scratch = [pltpu.VMEM((count, 2 * kv_width), jnp.bfloat16)]

    def scores(places, key_blocks):
        return pl.pallas_call(
            functools.partial(scores_kernel, places),
            out_shape=(
                jax.ShapeDtypeStruct((count * width // HEAD_DIM, count), jnp.bfloat16),
                jax.ShapeDtypeStruct((count, LANES), jnp.float32),
            ),
            in_specs=[SMEM] + [VMEM] * (1 + len(places)),
            out_specs=(VMEM,) * 2,
            scratch_shapes=[pltpu.VMEM(keys.shape, jnp.bfloat16)],
            compiler_params=params(8),
            cost_estimate=cost(8 * count * count * width),
            name="scores_" + "".join(str(p) for p in places),
        )(place, queries, *key_blocks)

    weights, prompt_peak = scores((2,), (keys_2,))
    out, aux = pl.pallas_call(
        middle_kernel,
        out_shape=(out_shape, jax.ShapeDtypeStruct((reached, 3 * width), jnp.float32)),
        in_specs=[SMEM] + [VMEM] * 4,
        out_specs=(HBM, VMEM),
        scratch_shapes=wide_scratch + out_scratch,
        compiler_params=params(8),
        cost_estimate=cost(1),
        name="middle",
    )(place, weights, two_left, state, prompt_peak)
    weights, prompt_peak = scores((3, 1), (keys_3, keys_1))
    return pl.pallas_call(
        last_kernel,
        out_shape=out_shape,
        in_specs=[SMEM] + [VMEM] * 8 + [HBM],
        out_specs=HBM,
        scratch_shapes=wide_scratch + tail_scratch + out_scratch,
        input_output_aliases={9: 0},
        compiler_params=params(10),
        cost_estimate=cost(1),
        name="last",
    )(place, queries, weights, one_left, values_3, segment_ids, state, prompt_peak, aux, out)


def attend_block(
    running,
    key_block,
    value_block,
    segment_block,
    first_row,
    query_heads,
    query_places,
    query_segment,
):
    number = key_block.shape[0]
    heads_here = key_block.shape[1] // HEAD_DIM
    key_places = first_row + jnp.arange(number, dtype=jnp.int32)
    same = (segment_block[None, :] == query_segment[:, None]) | (segment_block[None, :] == 0)
    visible = (key_places[None, :] <= query_places[:, None]) & same
    key_heads = key_block.reshape(number, heads_here, HEAD_DIM)
    value_heads = value_block.reshape(number, heads_here, HEAD_DIM)

    def compute(state):
        row_peak, row_total, weighted = state
        scores = jnp.einsum(
            "qhgd,khd->hgqk", query_heads, key_heads, preferred_element_type=jnp.float32
        ) * HEAD_DIM ** (-0.5)
        scores = jnp.where(visible[None, None], scores, -1e30)
        new_peak = jnp.maximum(row_peak, jnp.max(scores, axis=-1))
        factor = jnp.exp(row_peak - new_peak)
        weights = jnp.where(visible[None, None], jnp.exp(scores - new_peak[..., None]), 0.0)
        new_total = row_total * factor + jnp.sum(weights, axis=-1)
        added = jnp.einsum(
            "hgqk,khd->hgqd",
            weights.astype(jnp.bfloat16),
            value_heads,
            preferred_element_type=jnp.float32,
        )
        return (new_peak, new_total, weighted * factor[..., None] + added)

    return lax.cond(jnp.any(visible), compute, lambda state: state, running)


def gathered_path(queries, keys, values, segment_ids):
    row_count = queries.shape[0]
    heads_here = keys.shape[1] // HEAD_DIM
    my_index = lax.axis_index("ctx")
    query_places = my_index * row_count + jnp.arange(row_count, dtype=jnp.int32)
    query_heads = queries.reshape(row_count, heads_here, GROUP, HEAD_DIM)
    initial = (
        jnp.full((heads_here, GROUP, row_count), -1e30, jnp.float32),
        jnp.zeros((heads_here, GROUP, row_count), jnp.float32),
        jnp.zeros((heads_here, GROUP, row_count, HEAD_DIM), jnp.float32),
    )
    key_all = lax.all_gather(keys, "ctx", axis=0, tiled=True)
    value_all = lax.all_gather(values, "ctx", axis=0, tiled=True)
    segment_all = lax.all_gather(segment_ids, "ctx", axis=0, tiled=True)
    blocks = max(1, key_all.shape[0] // row_count)
    width_rows = key_all.shape[0] // blocks

    def turn(number, state):
        offset = number * width_rows
        key_part = lax.dynamic_slice_in_dim(key_all, offset, width_rows, 0)
        value_part = lax.dynamic_slice_in_dim(value_all, offset, width_rows, 0)
        segment_part = lax.dynamic_slice_in_dim(segment_all, offset, width_rows, 0)
        return attend_block(
            state, key_part, value_part, segment_part, offset, query_heads, query_places, segment_ids
        )

    row_peak, row_total, weighted = lax.fori_loop(0, blocks, turn, initial)
    mixed = weighted / row_total[..., None]
    mixed = jnp.transpose(mixed, (2, 0, 1, 3)).reshape(row_count, heads_here * GROUP * HEAD_DIM)
    return mixed.astype(jnp.bfloat16)


def per_device(parts, queries, keys, values, segment_ids):
    rows = queries.shape[0]
    tokens = rows * parts
    prompt, chain = tokens // 4, tokens // 8
    if parts == 4 and prompt == rows and 2 * chain == rows and rows % ROWS == 0 and keys.shape[1] >= max(chain, 2 * HEAD_DIM):
        return prompt_block_path(queries, keys, values, segment_ids)
    return gathered_path(queries, keys, values, segment_ids)


def solution(mesh):
    placed = (
        P(("groups", "ctx"), ("tp", "sub")),
        P(("groups", "ctx"), ("tp", "sub")),
        P(("groups", "ctx"), ("tp", "sub")),
        P(("groups", "ctx")),
    )
    return jax.shard_map(
        functools.partial(per_device, mesh.shape["ctx"]),
        mesh=mesh,
        in_specs=placed,
        out_specs=P(("groups", "ctx"), ("tp", "sub")),
        check_vma=False,
    )
```
